128 devices in a mesh: gx: 8 (over y_hi, x), gy: 16 (over y_lo, z, core).
Axes of the slice: x: 4, y: 4 (y_hi: 2, y_lo: 2; y = y_hi * 2 + y_lo), z: 4, core: 2. Of those that a mesh axis runs over, the one named last changes fastest.
Arguments:
- wave_old: float32 [256, 256, 1024], P('gx', 'gy'), may hold values from 3 to 9
- wave_now: float32 [256, 256, 1024], P('gx', 'gy'), may hold values from 3 to 9
- born_old: float32 [256, 256, 1024], P('gx', 'gy'), may hold values from -0.36 to 0.36
- born_now: float32 [256, 256, 1024], P('gx', 'gy'), may hold values from -0.36 to 0.36
- courant: float32 [256, 256, 1024], P('gx', 'gy'), may hold values from 0.04 to 0.18
- contrast: float32 [256, 256, 1024], P('gx', 'gy'), may hold values from -5 to 5
- src_cell: int32 [512], P(('gx', 'gy')), may hold values from 0 to 524287
- src_amp: float32 [512, 2], P(('gx', 'gy')), may hold values from -6 to 6
- rcv_cell: int32 [32768, 8], P(('gx', 'gy')), may hold values from 0 to 524287
- rcv_weight: float32 [32768, 8], P(('gx', 'gy')), may hold values from 0 to 1
- rcv_dest: int32 [32768, 1], P(('gx', 'gy')), may hold values from 0 to 127; in each aligned block of 256 rows (0 to 255, 256 to 511, ...) at most 4 rows name the same one
Outputs:
- wave_next: float32 [256, 256, 1024], P('gx', 'gy')
- wave_last: float32 [256, 256, 1024], P('gx', 'gy')
- born_next: float32 [256, 256, 1024], P('gx', 'gy')
- born_last: float32 [256, 256, 1024], P('gx', 'gy')
- gathers: float32 [128, 128, 2, 4], P(('gx', 'gy'))
The draws below stay inside these ranges and needn't reach their ends.
Inputs may be any that keep to these rules, and one draw needn't show every extreme that they name: `rcv_dest`: among the receivers of one device at most 4 name the same owner, and 4 is reached.
All inputs are finite; a program needn't handle non-finite values.
Results may differ from the reference program's by a relative error of at most 0.0003.
Values sent between devices are 32-bit elements; how exact they have to be, the bound alone decides.
No kernel may reach another device: no remote copies, remote signals or barrier semaphores. Data moves between devices by JAX's collectives and lax.ppermute only.
A program may use at most 128 MiB of HBM per device.

```python
import math
import jax
import jax.numpy as jnp
import numpy as np

CX = 32
CY = 16
NZ = 1024
CAP = 4
TAPS = 8
SRC_DEV = 4
NX = 256
NY = 256
R_DEV = 256
RCV = 32768
SRCS = 512
N_GY = 16
DEVICES = 128


def smooth_part(key, center_value, swing_size, ripple):
    keys = jax.random.split(key, 2)
    phases = jax.random.uniform(keys[0], (3,), jnp.float32, 0.0, 2.0 * math.pi)
    cycles = jax.random.randint(keys[1], (3,), 1, 3).astype(jnp.float32)
    pos_x = (jnp.arange(NX, dtype=jnp.float32) / NX)[:, None, None]
    pos_y = (jnp.arange(NY, dtype=jnp.float32) / NY)[None, :, None]
    pos_z = (jnp.arange(NZ, dtype=jnp.float32) / NZ)[None, None, :]
    along_x = jnp.sin(2.0 * math.pi * cycles[0] * pos_x + phases[0])
    along_y = jnp.cos(2.0 * math.pi * cycles[1] * pos_y + phases[1])
    along_z = jnp.sin(2.0 * math.pi * cycles[2] * pos_z + phases[2])
    return center_value + swing_size * along_x * along_y + ripple * along_z


def rough_normal(key):
    values = jax.random.normal(key, (NX, NY, NZ), jnp.float32)
    return jnp.clip(values, -5.0, 5.0) * 0.2


def draw_wave_old(key, part):
    own_key = jax.random.fold_in(key, 11)
    smooth_key, rough_key = jax.random.split(own_key)
    return (smooth_part(smooth_key, 6.0, 1.5, 0.5) + rough_normal(rough_key)).astype(jnp.float32)


def draw_wave_now(key, part):
    own_key = jax.random.fold_in(key, 23)
    smooth_key, rough_key = jax.random.split(own_key)
    return (smooth_part(smooth_key, 6.0, 1.5, 0.5) + rough_normal(rough_key)).astype(jnp.float32)


def set_ends(entries, rng, low, largest):
    longest = entries.shape.index(max(entries.shape))
    spots = []
    for shift in (0, 1):
        where = [jax.random.randint(jax.random.fold_in(rng, axis), (), 0, length) for axis, length in enumerate(entries.shape)]
        where[longest] = (where[longest] + shift) % entries.shape[longest]
        spots.append(tuple(where))
    return entries.at[spots[0]].set(low).at[spots[1]].set(largest)


def levels(key, shape, cuts, low, top_value):
    gain = 1.0
    for position, parts in cuts:
        heights = jax.random.uniform(jax.random.fold_in(jax.random.fold_in(key, 6), position), (parts,), jnp.float32, low / len(cuts), top_value / len(cuts))
        gain = gain * jnp.repeat(jnp.exp(heights), shape[position] // parts).reshape((-1,) + (1,) * (len(shape) - 1 - position))
    return gain


def shared_out(key, own, number, rows, amount, top, most, skew):
    ranking = jax.random.permutation(key, amount)
    packed, common = load_shares(amount, rows * top, most, skew, True), load_shares(amount, rows * top, most, skew, False)
    places = jnp.arange(amount)

    def named(tallies, offset_by):
        used = int((tallies > 0).sum())
        fixed = max(1, used // 4)
        moved = fixed + (places - fixed + offset_by * (used - fixed)) % max(1, amount - fixed)
        return jnp.zeros((amount,), jnp.int32).at[ranking[jnp.where(places < fixed, places, moved)]].set(jnp.asarray(tallies, jnp.int32))

    tallies = jnp.where(number % 4 == 0, named(packed, number // 4), named(common, number - number // 4 - 1))
    mixed = jax.random.permutation(jax.random.fold_in(own, 3), amount)
    giver, sink = mixed[0:amount // 2 * 2:2], mixed[1:amount // 2 * 2:2]
    room = jnp.minimum(tallies[giver] - 1, most - tallies[sink]) // 2
    room = jnp.where((giver == ranking[0]) | (sink == ranking[0]) | (tallies[sink] == 0), 0, jnp.maximum(room, 0))
    moved = jax.random.randint(jax.random.fold_in(own, 4), (amount // 2,), 0, 1 << 20) % (room + 1)
    tallies = tallies.at[giver].add(-moved).at[sink].add(moved)
    labels = jnp.searchsorted(jnp.cumsum(tallies), jnp.arange(rows * top), side="right").astype(jnp.int32)
    table = labels.reshape(top, rows).T
    table = table[jax.random.permutation(jax.random.fold_in(own, 1), rows)]
    offset_by = jax.random.randint(jax.random.fold_in(own, 2), (rows, 1), 0, top)
    return jnp.take_along_axis(table, (jnp.arange(top)[None, :] + offset_by) % top, axis=1)


def load_shares(amount, total, bound, skew, full):
    weights = [(1 << 20) // math.isqrt(grade ** skew) + 1 for grade in range(1, amount + 1)]
    largest = bound if full else min(bound, max(-(-total // amount), total * weights[0] // sum(weights)))
    least = 1 if total - largest >= amount - 1 else 0
    counts, surplus = [largest] + [least] * (amount - 1), total - largest - least * (amount - 1)
    while surplus > 0:
        free = [i for i in range(1, amount) if counts[i] < largest] or [i for i in range(1, amount) if counts[i] < bound]
        pool, budget = sum([weights[i] for i in free]), surplus
        for i in free:
            addition = min(bound - counts[i], max(1, budget * weights[i] // pool), surplus)
            counts[i] = counts[i] + addition
            surplus = surplus - addition
    return np.array(counts)


def centred(key, extent, spread, limit, pieces=(), kind=jnp.bfloat16):
    gain = levels(key, extent, pieces, -0.22, 0.18) if pieces else 1.0
    drawn = jax.random.normal(key, extent, jnp.float32) * spread * gain
    return jnp.minimum(jnp.maximum(drawn, -limit), limit).astype(kind)


def setup_inputs(seed: int = 0) -> dict:
    key_list = jax.random.split(jax.random.key(seed), 12)
    wave_old = draw_wave_old(jax.random.fold_in(key_list[11], 71), 0)
    wave_now = draw_wave_now(jax.random.fold_in(key_list[11], 71), 0)
    born_old = centred(key_list[2], (NX, NY, NZ), 0.06, 0.36, ((0, 8), (1, 16)), jnp.float32)
    born_now = centred(key_list[3], (NX, NY, NZ), 0.06, 0.36, ((0, 8), (1, 16)), jnp.float32)
    courant = jnp.clip(jnp.exp(math.log(0.18) - 1.50407746 * jax.random.uniform(key_list[4], (NX, NY, NZ), jnp.float32) ** levels(key_list[4], (NX, NY, NZ), ((0, 8), (1, 16)), -0.2, 0.2)), 0.04, 0.18)
    contrast = centred(key_list[5], (NX, NY, NZ), 1.0, 5.0, ((0, 8), (1, 16)), jnp.float32)
    src_cell = set_ends(jax.random.randint(key_list[6], (SRCS,), 0, CX * CY * NZ), jax.random.fold_in(key_list[6], 1), 0, (CX * CY * NZ) - 1).astype(jnp.int32)
    src_amp = centred(key_list[7], (SRCS, 2), 1.0, 6.0, ((0, 128),), jnp.float32)
    rcv_cell = set_ends(jax.random.randint(key_list[8], (RCV, TAPS), 0, CX * CY * NZ), jax.random.fold_in(key_list[8], 1), 0, (CX * CY * NZ) - 1).astype(jnp.int32)
    rcv_weight = jnp.clip(1.0 * jax.random.uniform(key_list[9], (RCV, TAPS), jnp.float32) ** levels(key_list[9], (RCV, TAPS), ((0, 128),), -0.2, 0.2), 0.0, 1.0)
    rcv_dest_keys = jax.random.split(jax.random.fold_in(key_list[10], 1), RCV // R_DEV)
    rcv_dest_turns = jax.random.permutation(jax.random.fold_in(key_list[10], 3), RCV // R_DEV)
    rcv_dest = jax.vmap(lambda own, number: shared_out(jax.random.fold_in(key_list[10], 2), own, number, R_DEV, DEVICES, 1, CAP, 2))(rcv_dest_keys, rcv_dest_turns).reshape((RCV, 1))
    return dict(wave_old=wave_old, wave_now=wave_now, born_old=born_old, born_now=born_now, courant=courant, contrast=contrast, src_cell=src_cell, src_amp=src_amp, rcv_cell=rcv_cell, rcv_weight=rcv_weight, rcv_dest=rcv_dest)


CENTER = -205.0 / 72.0
WEIGHTS = (8.0 / 5.0, -1.0 / 5.0, 8.0 / 315.0, -1.0 / 560.0)


def laplace(padded, count_x, count_y):
    depth = padded.shape[2]
    padded_z = jnp.pad(padded, ((0, 0), (0, 0), (4, 4)))
    middle = padded_z[4:4 + count_x, 4:4 + count_y, 4:4 + depth]
    summed = (3.0 * CENTER) * middle
    for k in range(1, 5):
        near = padded_z[4 + k:4 + k + count_x, 4:4 + count_y, 4:4 + depth] + padded_z[4 - k:4 - k + count_x, 4:4 + count_y, 4:4 + depth]
        near = near + padded_z[4:4 + count_x, 4 + k:4 + k + count_y, 4:4 + depth] + padded_z[4:4 + count_x, 4 - k:4 - k + count_y, 4:4 + depth]
        near = near + padded_z[4:4 + count_x, 4:4 + count_y, 4 + k:4 + k + depth] + padded_z[4:4 + count_x, 4:4 + count_y, 4 - k:4 - k + depth]
        summed = summed + WEIGHTS[k - 1] * near
    return summed


def global_lap(field):
    padded = jnp.pad(field, ((4, 4), (4, 4), (0, 0)))
    return laplace(padded, field.shape[0], field.shape[1])


def global_index(cells, owner):
    block_x = owner // N_GY
    block_y = owner % N_GY
    local_x = cells // (CY * NZ)
    local_y = (cells // NZ) % CY
    local_z = cells % NZ
    return block_x * CX + local_x, block_y * CY + local_y, local_z


def reference(wave_old, wave_now, born_old, born_now, courant, contrast, src_cell, src_amp, rcv_cell, rcv_weight, rcv_dest):
    src_owner = (jnp.arange(SRCS) // SRC_DEV).astype(jnp.int32)
    pos_x, pos_y, pos_z = global_index(src_cell, src_owner)
    source_one = jnp.zeros(wave_now.shape, jnp.float32).at[pos_x, pos_y, pos_z].add(src_amp[:, 0])
    source_two = jnp.zeros(wave_now.shape, jnp.float32).at[pos_x, pos_y, pos_z].add(src_amp[:, 1])
    wave_next = (2.0 * wave_now - wave_old) + courant * global_lap(wave_now) + source_one
    wave_last = (2.0 * wave_next - wave_now) + courant * global_lap(wave_next) + source_two
    accel_one = (wave_next - 2.0 * wave_now) + wave_old
    accel_two = (wave_last - 2.0 * wave_next) + wave_now
    born_next = (2.0 * born_now - born_old) + courant * global_lap(born_now) + contrast * accel_one
    born_last = (2.0 * born_next - born_now) + courant * global_lap(born_next) + contrast * accel_two
    rcv_owner = (jnp.arange(RCV) // R_DEV).astype(jnp.int32)
    cell_x, cell_y, cell_z = global_index(rcv_cell, rcv_owner[:, None])
    sample_one = jnp.sum(rcv_weight * born_next[cell_x, cell_y, cell_z], axis=1)
    sample_two = jnp.sum(rcv_weight * born_last[cell_x, cell_y, cell_z], axis=1)
    samples = jnp.stack([sample_one, sample_two], axis=1)
    dest = rcv_dest[:, 0].reshape(DEVICES, R_DEV)
    onehot = (dest[:, :, None] == jnp.arange(DEVICES, dtype=jnp.int32)[None, None, :]).astype(jnp.int32)
    before = jnp.cumsum(onehot, axis=1) - onehot
    slot = jnp.sum(before * onehot, axis=2).reshape(-1).astype(jnp.int32)
    gathers = jnp.zeros((DEVICES, DEVICES, 2, CAP), jnp.float32).at[rcv_dest[:, 0], rcv_owner, :, slot].set(samples)
    return wave_next, wave_last, born_next, born_last, gathers
```

```python
import functools

import jax
import jax.numpy as jnp
from jax import lax
from jax.experimental import pallas as pl
from jax.experimental.pallas import tpu as pltpu
from jax.sharding import PartitionSpec as P

CAP = 4
CENTER = -205.0 / 72.0
WEIGHTS = (8.0 / 5.0, -1.0 / 5.0, 8.0 / 315.0, -1.0 / 560.0)
CX, CY, NZ = 32, 16, 1024
TZ = NZ // 128
BLOCK = (CX, CY, NZ)
XFACE = (8, CY, NZ)
YFACE = (CX, 8, NZ)
F32 = jnp.float32


def iotas():
    sub = lax.broadcasted_iota(jnp.int32, (8, 128), 0)
    lane = lax.broadcasted_iota(jnp.int32, (8, 128), 1)
    return sub, lane


def tile(ref, x, t, z):
    return ref[x, t * 8 : t * 8 + 8, z * 128 : z * 128 + 128]


def put(ref, x, t, z, value):
    ref[x, t * 8 : t * 8 + 8, z * 128 : z * 128 + 128] = value


def pack_y(sub, even, ya, yb, x, z, w0, w1, b0, b1):
    low = jnp.where(sub < 4, w0, pltpu.roll(b0, 4, 0))
    high = jnp.where(sub < 4, pltpu.roll(w1, 4, 0), b1)
    put(ya, x, 0, z, jnp.where(even, high, low))
    put(yb, x, 0, z, jnp.where(even, low, high))


def pack_x(even, xa, xb, wave, born):
    start_a = jnp.where(even, CX - 4, 0)
    start_b = jnp.where(even, 0, CX - 4)
    for i in range(4):
        xa[i] = wave[start_a + i]
        xa[i + 4] = born[start_a + i]
        xb[i] = wave[start_b + i]
        xb[i + 4] = born[start_b + i]


def pack_kernel(place, wave, born, xa, xb, ya, yb):
    sub, _ = iotas()
    even_y = place[1] == 0
    pack_x(place[0] == 0, xa, xb, wave, born)

    def step(x, carry):
        for z in range(TZ):
            pack_y(
                sub, even_y, ya, yb, x, z,
                tile(wave, x, 0, z), tile(wave, x, 1, z), tile(born, x, 0, z), tile(born, x, 1, z),
            )
        return carry

    lax.fori_loop(0, CX, step, 0)


def laplace_rows(ref, x, spots, sub, lane):
    rows = [[tile(ref, x, t, z) for z in range(TZ)] for t in range(2)]
    made = {}

    def turned(t, z, shift, axis):
        shift = shift % (8, 128)[axis]
        if shift == 0:
            return rows[t][z]
        key = (t, z, shift, axis)
        if key not in made:
            made[key] = pltpu.roll(rows[t][z], shift, axis)
        return made[key]

    sums = [[None] * TZ for _ in range(2)]
    for z in range(TZ):
        for t in range(2):
            total = 3.0 * CENTER * rows[t][z]
            for k in range(1, 5):
                near = None
                for s in (k, -k):
                    if s in spots:
                        value = tile(ref, x + s, t, z)
                        near = value if near is None else near + value
                ahead = turned(1, z, -k, 0) if t == 0 else 0.0
                up = jnp.where(sub < 8 - k, turned(t, z, -k, 0), ahead)
                behind = turned(0, z, k, 0) if t == 1 else 0.0
                down = jnp.where(sub >= k, turned(t, z, k, 0), behind)
                ahead = turned(t, z + 1, -k, 1) if z + 1 < TZ else 0.0
                right = jnp.where(lane < 128 - k, turned(t, z, -k, 1), ahead)
                behind = turned(t, z - 1, k, 1) if z > 0 else 0.0
                left = jnp.where(lane >= k, turned(t, z, k, 1), behind)
                flat = (up + down) + (right + left)
                near = flat if near is None else near + flat
                total = total + WEIGHTS[k - 1] * near
            sums[t][z] = total
    return rows, sums


def inner_kernel(cells, amps, wave, wave_old, born, born_old, courant, contrast, wave_part, born_part):
    sub, lane = iotas()

    def one(x, spots):
        rows, sums = laplace_rows(wave, x, spots, sub, lane)
        speed = [[tile(courant, x, t, z) for z in range(TZ)] for t in range(2)]
        for t in range(2):
            for z in range(TZ):
                moved = speed[t][z] * sums[t][z]
                put(wave_part, x, t, z, (2.0 * rows[t][z] - tile(wave_old, x, t, z)) + moved)
                put(born_part, x, t, z, tile(contrast, x, t, z) * moved - tile(born_old, x, t, z))
        rows, sums = laplace_rows(born, x, spots, sub, lane)
        for t in range(2):
            for z in range(TZ):
                moved = 2.0 * rows[t][z] + tile(courant, x, t, z) * sums[t][z]
                put(born_part, x, t, z, tile(born_part, x, t, z) + moved)

    def spots_of(x):
        return {s for s in range(-4, 5) if s and 0 <= x + s < CX}

    for x in range(4):
        one(x, spots_of(x))
    lax.fori_loop(4, CX - 4, lambda x, carry: (one(x, spots_of(8)), carry)[1], 0)
    for x in range(CX - 4, CX):
        one(x, spots_of(x))

    for i in range(4):
        cell = cells[i]
        x = lax.shift_right_logical(cell, 14)
        y = lax.bitwise_and(lax.shift_right_logical(cell, 10), 15)
        z = lax.bitwise_and(cell, NZ - 1)
        row = pl.multiple_of(lax.bitwise_and(y, 8), 8)
        col = pl.multiple_of(lax.bitwise_and(z, NZ - 128), 128)
        here = (sub == lax.bitwise_and(y, 7)) & (lane == lax.bitwise_and(z, 127))
        added = jnp.where(here, amps[i], 0.0)
        at = (x, pl.ds(row, 8), pl.ds(col, 128))
        wave_part[at] = wave_part[at] + added
        born_part[at] = born_part[at] + contrast[at] * added


def fix(place, wave_part, born_part, courant, contrast, xa, xb, ya, yb, wave, born, grid, faces):
    sub, _ = iotas()
    even_x = place[0] == 0
    even_y = place[1] == 0
    low_weights = [jnp.where(sub < k, WEIGHTS[k - 1], 0.0) for k in range(1, 5)]
    high_weights = [jnp.where(sub >= 8 - k, WEIGHTS[k - 1], 0.0) for k in range(1, 5)]

    def turned(value, shift):
        shift = shift % 8
        return value if shift == 0 else pltpu.roll(value, shift, 0)

    def weighted(weights, values):
        total = weights[0] * values[0]
        for w, v in zip(weights[1:], values[1:]):
            total = total + w * v
        return total

    def one(x, side, offset):
        for z in range(TZ):
            from_a, from_b = tile(ya, x, 0, z), tile(yb, x, 0, z)
            low = jnp.where(even_y, from_b, from_a)
            high = jnp.where(even_y, from_a, from_b)
            lows = [turned(low, s) for s in range(8)]
            highs = [turned(high, s) for s in range(8)]
            wave_sums = [
                weighted(low_weights, [lows[(4 + k) % 8] for k in range(1, 5)]),
                weighted(high_weights, [highs[(8 - k) % 8] for k in range(1, 5)]),
            ]
            born_sums = [
                weighted(low_weights, [lows[k] for k in range(1, 5)]),
                weighted(high_weights, [highs[(4 - k) % 8] for k in range(1, 5)]),
            ]
            finals = []
            for t in range(2):
                wave_sum, born_sum = wave_sums[t], born_sums[t]
                if side:
                    for m in range(4):
                        reach = offset + 4 - m if side < 0 else 4 - offset + m
                        if 1 <= reach <= 4:
                            lone, other = (xb, xa) if side < 0 else (xa, xb)
                            w = WEIGHTS[reach - 1]
                            wave_sum = wave_sum + w * jnp.where(even_x, tile(lone, m, t, z), tile(other, m, t, z))
                            born_sum = born_sum + w * jnp.where(even_x, tile(lone, m + 4, t, z), tile(other, m + 4, t, z))
                speed = tile(courant, x, t, z)
                moved = speed * wave_sum
                wave_value = tile(wave_part, x, t, z) + moved
                born_value = tile(born_part, x, t, z) + (tile(contrast, x, t, z) * moved + speed * born_sum)
                put(wave, x, t, z, wave_value)
                put(born, x, t, z, born_value)
                grid[pl.ds(pl.multiple_of(x * 128 + t * 64 + z * 8, 8), 8), :] = born_value
                finals.append((wave_value, born_value))
            if faces is not None:
                (w0, b0), (w1, b1) = finals
                pack_y(sub, even_y, faces[2], faces[3], x, z, w0, w1, b0, b1)

    for x in range(4):
        one(x, -1, x)
    lax.fori_loop(4, CX - 4, lambda x, carry: (one(x, 0, 0), carry)[1], 0)
    for x in range(CX - 4, CX):
        one(x, 1, x - (CX - 4))
    if faces is not None:
        pack_x(even_x, faces[0], faces[1], wave, born)


def fix_kernel(
    place, wave_part, born_part, courant, contrast, rxa, rxb, rya, ryb, wave, born, grid, xa, xb, ya, yb
):
    fix(place, wave_part, born_part, courant, contrast, rxa, rxb, rya, ryb, wave, born, grid, (xa, xb, ya, yb))


def take(rows_at, grid, picks, rows, out):
    def step(g, carry):
        for j in range(4):
            r = g * 4 + j
            for t in range(8):
                rows[pl.ds(r * 8 + t, 1), :] = grid[pl.ds(rows_at[t, r], 1), :]
        return carry

    lax.fori_loop(0, 64, step, 0)

    def total(g, carry):
        part = pl.ds(pl.multiple_of(g * 256, 256), 256)
        value = (rows[part, :] * picks[part, :]).reshape(32, 8, 128)
        out[pl.ds(pl.multiple_of(g * 32, 32), 32), :] = jnp.sum(value, axis=1)
        return carry

    lax.fori_loop(0, 8, total, 0)


def take_kernel(rows_at, grid, picks, out, rows):
    take(rows_at, grid, picks, rows, out)


def last_kernel(
    place, rows_at, wave_part, born_part, courant, contrast, rxa, rxb, rya, ryb,
    picks, first, slots, dest, wave, born, packed, grid, rows, sums,
):
    fix(place, wave_part, born_part, courant, contrast, rxa, rxb, rya, ryb, wave, born, grid, None)
    take(rows_at, grid, picks, rows, sums)
    one = jnp.sum(first[...], axis=1, keepdims=True)
    two = jnp.sum(sums[...], axis=1, keepdims=True)
    lane = lax.broadcasted_iota(jnp.int32, (256, 128), 1)
    spread = jnp.where(lane < 4, one, two) * slots[...]
    owner = lax.broadcasted_iota(jnp.int32, (128, 256), 0)
    chosen = jnp.where(owner == dest[...], 1.0, 0.0).astype(F32)
    packed[...] = jnp.dot(chosen, spread, precision=lax.Precision.HIGHEST, preferred_element_type=F32)


def pairs(count, first):
    found = []
    for i in range(first, count - 1, 2):
        found += [(i, i + 1), (i + 1, i)]
    return found


VM = pl.BlockSpec(memory_space=pltpu.VMEM)
SM = pl.BlockSpec(memory_space=pltpu.SMEM)


def call(kernel, name, args, smem, outs, scratch=(), us=5):
    return pl.pallas_call(
        kernel,
        name=name,
        out_shape=tuple(jax.ShapeDtypeStruct(s, F32) for s in outs),
        in_specs=[SM] * smem + [VM] * (len(args) - smem),
        out_specs=tuple([VM] * len(outs)),
        scratch_shapes=list(scratch),
        compiler_params=pltpu.CompilerParams(vmem_limit_bytes=48 * 1024 * 1024),
        cost_estimate=pl.CostEstimate(flops=0, bytes_accessed=us * 3_000_000, transcendentals=0),
    )(*args)


def exchange(faces):
    xa, xb, ya, yb = faces
    ryb = lax.ppermute(yb, "gy", pairs(16, 1))
    rxb = lax.ppermute(xb, "gx", pairs(8, 1))
    rxa = lax.ppermute(xa, "gx", pairs(8, 0))
    rya = lax.ppermute(ya, "gy", pairs(16, 0))
    return rxa, rxb, rya, ryb


def body(
    wave_old,
    wave_now,
    born_old,
    born_now,
    courant,
    contrast,
    src_cell,
    src_amp,
    rcv_cell,
    rcv_weight,
    rcv_dest,
):
    face_shapes = (XFACE, XFACE, YFACE, YFACE)
    place = jnp.stack([lax.axis_index("gx") % 2, lax.axis_index("gy") % 2]).astype(jnp.int32)

    faces = call(pack_kernel, "pack", (place, wave_now, born_now), 1, face_shapes, us=2)
    halo = exchange(faces)
    parts = call(
        inner_kernel,
        "inner1",
        (src_cell, src_amp[:, 0], wave_now, wave_old, born_now, born_old, courant, contrast),
        2,
        (BLOCK, BLOCK),
        us=10,
    )

    cell = rcv_cell.T
    rows_at = (
        ((cell >> 14) << 7) | (((cell >> 13) & 1) << 6) | (((cell >> 7) & 7) << 3) | ((cell >> 10) & 7)
    )
    lane = lax.broadcasted_iota(jnp.int32, (256, 8, 128), 2)
    picks = jnp.where(lane == (rcv_cell & 127)[:, :, None], rcv_weight[:, :, None], 0.0).reshape(2048, 128)
    dest = rcv_dest[:, 0]
    order = jnp.arange(256, dtype=jnp.int32)
    earlier = (dest[:, None] == dest[None, :]) & (order[None, :] < order[:, None])
    slot = jnp.sum(earlier.astype(jnp.int32), axis=1)
    lane = lax.broadcasted_iota(jnp.int32, (256, 128), 1)
    slots = jnp.where((lane < 8) & (lane % 4 == slot[:, None]), 1.0, 0.0).astype(F32)

    wave_next, born_next, grid, *faces = call(
        fix_kernel,
        "fix1",
        (place, *parts, courant, contrast, *halo),
        1,
        (BLOCK, BLOCK, (4096, 128)) + face_shapes,
        us=4,
    )
    halo = exchange(faces)
    parts = call(
        inner_kernel,
        "inner2",
        (src_cell, src_amp[:, 1], wave_next, wave_now, born_next, born_now, courant, contrast),
        2,
        (BLOCK, BLOCK),
        us=10,
    )
    (first,) = call(
        take_kernel, "take1", (rows_at, grid, picks), 1, ((256, 128),), [pltpu.VMEM((2048, 128), F32)], us=4
    )
    wave_last, born_last, packed = call(
        last_kernel,
        "last",
        (place, rows_at, *parts, courant, contrast, *halo, picks, first, slots, dest[None, :]),
        2,
        (BLOCK, BLOCK, (128, 128)),
        [pltpu.VMEM((4096, 128), F32), pltpu.VMEM((2048, 128), F32), pltpu.VMEM((256, 128), F32)],
        us=8,
    )
    arrived = lax.all_to_all(
        packed.reshape(128, 1, 128), ("gx", "gy"), split_axis=0, concat_axis=0, tiled=True
    )
    gathers = arrived[:, 0, :8].reshape(1, 128, 2, CAP)
    return (wave_next, wave_last, born_next, born_last, gathers)


def solution(mesh):
    placed = (P("gx", "gy", None),) * 6 + (
        P(("gx", "gy")),
        P(("gx", "gy"), None),
        P(("gx", "gy"), None),
        P(("gx", "gy"), None),
        P(("gx", "gy"), None),
    )
    return jax.shard_map(
        body,
        mesh=mesh,
        in_specs=placed,
        out_specs=(P("gx", "gy", None),) * 4 + (P(("gx", "gy"), None, None, None),),
        check_vma=False,
    )
```

```python
import jax
import jax.numpy as jnp
from jax import lax
from jax.experimental import pallas as pl
from jax.experimental.pallas import tpu as pltpu
from jax.sharding import PartitionSpec as P

CAP = 4
SCALE = 5040.0
CENTER = -3.0 * 14350.0
WEIGHTS = (8064.0, -1008.0, 128.0, -9.0)
CX, CY, NZ = 32, 16, 1024
TZ = NZ // 128
BLOCK = (CX, CY, NZ)
XFACE = (8, CY, NZ)
YFACE = (CX, 8, NZ)
STRIP = 24
LAYER = TZ * STRIP
ROWS = (CX + 8) * LAYER + 8
F32 = jnp.float32
BF16 = jnp.bfloat16


def iotas():
    sub = lax.broadcasted_iota(jnp.int32, (8, 128), 0)
    lane = lax.broadcasted_iota(jnp.int32, (8, 128), 1)
    return sub, lane


def tile(ref, x, t, z):
    return ref[x, t * 8 : t * 8 + 8, z * 128 : z * 128 + 128]


def put(ref, x, t, z, value):
    ref[x, t * 8 : t * 8 + 8, z * 128 : z * 128 + 128] = value


def strip(x, t, z, shift=0):
    return pl.ds(x * LAYER + (4 * LAYER + z * STRIP + 8 + t * 8 + shift), 8)


def clear(*refs):
    zero = jnp.zeros((8, 128), F32)

    def gaps(x, carry):
        for z in range(TZ):
            for ref in refs:
                ref[pl.ds(pl.multiple_of(x * LAYER + z * STRIP, 8), 8), :] = zero
        return carry

    def layer(i, carry):
        x = jnp.where(i < 4, i, i + CX)
        for z in range(TZ):
            for t in range(2):
                for ref in refs:
                    ref[pl.ds(pl.multiple_of(x * LAYER + z * STRIP + 8 + t * 8, 8), 8), :] = zero
        return carry

    lax.fori_loop(0, CX + 8, gaps, 0)
    lax.fori_loop(0, 8, layer, 0)
    for ref in refs:
        ref[pl.ds(ROWS - 8, 8), :] = zero


def pack_y(sub, even, ya, yb, x, z, w0, w1, b0, b1):
    low = jnp.where(sub < 4, w0, pltpu.roll(b0, 4, 0))
    high = jnp.where(sub < 4, pltpu.roll(w1, 4, 0), b1)
    put(ya, x, 0, z, jnp.where(even, high, low))
    put(yb, x, 0, z, jnp.where(even, low, high))


def pack_x(even, xa, xb, wave, born):
    start_a = jnp.where(even, CX - 4, 0)
    start_b = jnp.where(even, 0, CX - 4)
    for i in range(4):
        xa[i] = wave[start_a + i]
        xa[i + 4] = born[start_a + i]
        xb[i] = wave[start_b + i]
        xb[i + 4] = born[start_b + i]


def pack_kernel(place, wave_in, born_in, wave_rows, born_rows, xa, xb, ya, yb, wave, born, sems):
    sub, _ = iotas()
    even_y = place[1] == 0
    parts = 4
    each = CX // parts

    def copies(c):
        part = pl.ds(c * each, each)
        return (
            pltpu.make_async_copy(wave_in.at[part], wave.at[part], sems.at[0, c]),
            pltpu.make_async_copy(born_in.at[part], born.at[part], sems.at[1, c]),
        )

    for c in range(parts):
        for copy in copies(c):
            copy.start()
    clear(wave_rows, born_rows)
    for c in range(parts):
        for copy in copies(c):
            copy.wait()

        def step(x, carry):
            for z in range(TZ):
                w0, w1, b0, b1 = tile(wave, x, 0, z), tile(wave, x, 1, z), tile(born, x, 0, z), tile(born, x, 1, z)
                pack_y(sub, even_y, ya, yb, x, z, w0, w1, b0, b1)
                wave_rows[strip(x, 0, z), :] = w0
                wave_rows[strip(x, 1, z), :] = w1
                born_rows[strip(x, 0, z), :] = b0
                born_rows[strip(x, 1, z), :] = b1
            return carry

        lax.fori_loop(c * each, (c + 1) * each, step, 0)
    pack_x(place[0] == 0, xa, xb, wave, born)


def along_z(ref, high, low, table, out):
    zero = jnp.zeros((CX * CY, 128), BF16)
    for half in (high, low):
        half[:, 0:128] = zero
        half[:, 128 + NZ : 256 + NZ] = zero

    def split(x, carry):
        rows = pl.ds(pl.multiple_of(x * CY, CY), CY)
        for z in range(TZ):
            value = ref[pl.ds(pl.multiple_of(x * LAYER + (4 * LAYER + z * STRIP + 8), 8), CY), :]
            top = value.astype(BF16)
            high[rows, 128 + z * 128 : 256 + z * 128] = top
            low[rows, 128 + z * 128 : 256 + z * 128] = (value - top.astype(F32)).astype(BF16)
        return carry

    lax.fori_loop(0, CX, split, 0, unroll=2)
    for c in range(NZ // 256):
        window = slice(c * 256, c * 256 + 512)
        both = jnp.concatenate([high[:, window], low[:, window]], axis=1)
        out[:, c * 256 : c * 256 + 256] = jnp.dot(both, table[...], preferred_element_type=F32)


def spread(ref, z_sum, x, t, z):
    here = ref[strip(x, t, z), :]
    total = CENTER * here + z_sum[pl.ds(pl.multiple_of(x * CY + t * 8, 8), 8), z * 128 : z * 128 + 128]
    for k in range(1, 5):
        flat = ref[strip(x, t, z, k), :] + ref[strip(x, t, z, -k), :]
        deep = ref[strip(x, t, z, k * LAYER), :] + ref[strip(x, t, z, -k * LAYER), :]
        total = total + WEIGHTS[k - 1] * (flat + deep)
    return here, total


def add_sources(cells, amps, contrast, wave_part, born_part):
    sub, lane = iotas()
    for i in range(4):
        cell = cells[i]
        x = lax.shift_right_logical(cell, 14)
        y = lax.bitwise_and(lax.shift_right_logical(cell, 10), 15)
        z = lax.bitwise_and(cell, NZ - 1)
        row = pl.multiple_of(lax.bitwise_and(y, 8), 8)
        col = pl.multiple_of(lax.bitwise_and(z, NZ - 128), 128)
        here = (sub == lax.bitwise_and(y, 7)) & (lane == lax.bitwise_and(z, 127))
        added = jnp.where(here, amps[i], 0.0)
        at = (x, pl.ds(row, 8), pl.ds(col, 128))
        wave_part[at] = wave_part[at] + added
        born_part[at] = born_part[at] + contrast[at] * added


def inner_first(
    cells, amps, wave, born, table, wave_old_in, born_old_in, courant_in, contrast_in,
    wave_part, born_part, courant, contrast, wave_old, born_old, high, low, wave_z, born_z, sems,
):
    copies = [
        pltpu.make_async_copy(a, b, sems.at[i])
        for i, (a, b) in enumerate(
            ((wave_old_in, wave_old), (born_old_in, born_old), (courant_in, courant), (contrast_in, contrast))
        )
    ]
    for copy in copies:
        copy.start()
    along_z(wave, high, low, table, wave_z)
    along_z(born, high, low, table, born_z)
    for copy in copies:
        copy.wait()

    def step(x, carry):
        for z in range(TZ):
            for t in range(2):
                speed = tile(courant, x, t, z) * (1.0 / SCALE)
                put(courant, x, t, z, speed)
                here, total = spread(wave, wave_z, x, t, z)
                moved = speed * total
                put(wave_part, x, t, z, (2.0 * here - tile(wave_old, x, t, z)) + moved)
                here, total = spread(born, born_z, x, t, z)
                moved = speed * total + tile(contrast, x, t, z) * moved
                put(born_part, x, t, z, (2.0 * here - tile(born_old, x, t, z)) + moved)
        return carry

    lax.fori_loop(0, CX, step, 0)
    add_sources(cells, amps, contrast, wave_part, born_part)


def inner_second(
    cells, amps, rows_at, wave, born, table, wave_old, born_old, courant, contrast, picks, wave_now, born_now,
    wave_part, born_part, first, wave_out, born_out, high, low, wave_z, born_z, rows, sems,
):
    copies = [
        pltpu.make_async_copy(wave_now, wave_out, sems.at[0]),
        pltpu.make_async_copy(born_now, born_out, sems.at[1]),
    ]
    for copy in copies:
        copy.start()
    along_z(wave, high, low, table, wave_z)
    along_z(born, high, low, table, born_z)

    def step(x, carry):
        for z in range(TZ):
            for t in range(2):
                speed = tile(courant, x, t, z)
                here, total = spread(wave, wave_z, x, t, z)
                moved = speed * total
                put(wave_part, x, t, z, (2.0 * here - wave_old[strip(x, t, z), :]) + moved)
                here, total = spread(born, born_z, x, t, z)
                moved = speed * total + tile(contrast, x, t, z) * moved
                put(born_part, x, t, z, (2.0 * here - born_old[strip(x, t, z), :]) + moved)
        return carry

    lax.fori_loop(0, CX, step, 0)
    add_sources(cells, amps, contrast, wave_part, born_part)
    take(rows_at, born, picks, rows, first)
    for copy in copies:
        copy.wait()


def fix(place, wave_part, born_part, courant, contrast, xa, xb, ya, yb, wave, born, wave_rows, born_rows, faces):
    sub, _ = iotas()
    even_x = place[0] == 0
    even_y = place[1] == 0
    part = lax.bitwise_and(sub, 3)
    low_weights = [jnp.where(part < k, WEIGHTS[k - 1], 0.0) for k in range(1, 4)]
    high_weights = [jnp.where(part >= 4 - k, WEIGHTS[k - 1], 0.0) for k in range(1, 4)]

    def one(x, side, offset):
        for z in range(TZ):
            from_a, from_b = tile(ya, x, 0, z), tile(yb, x, 0, z)
            low = jnp.where(even_y, from_b, from_a)
            high = jnp.where(even_y, from_a, from_b)
            low_sum, high_sum = WEIGHTS[3] * low, WEIGHTS[3] * high
            for k in range(1, 4):
                low_sum = low_sum + low_weights[k - 1] * pltpu.roll(low, 4 + k, 0)
                high_sum = high_sum + high_weights[k - 1] * pltpu.roll(high, 4 - k, 0)
            wave_sums = [
                jnp.where(sub < 4, low_sum, 0.0),
                jnp.where(sub < 4, 0.0, pltpu.roll(high_sum, 4, 0)),
            ]
            born_sums = [
                jnp.where(sub < 4, pltpu.roll(low_sum, 4, 0), 0.0),
                jnp.where(sub < 4, 0.0, high_sum),
            ]
            finals = []
            for t in range(2):
                wave_sum, born_sum = wave_sums[t], born_sums[t]
                if side:
                    for m in range(4):
                        reach = offset + 4 - m if side < 0 else 4 - offset + m
                        if 1 <= reach <= 4:
                            lone, other = (xb, xa) if side < 0 else (xa, xb)
                            w = WEIGHTS[reach - 1]
                            wave_sum = wave_sum + w * jnp.where(even_x, tile(lone, m, t, z), tile(other, m, t, z))
                            born_sum = born_sum + w * jnp.where(even_x, tile(lone, m + 4, t, z), tile(other, m + 4, t, z))
                speed = tile(courant, x, t, z)
                moved = speed * wave_sum
                wave_value = tile(wave_part, x, t, z) + moved
                born_value = tile(born_part, x, t, z) + (tile(contrast, x, t, z) * moved + speed * born_sum)
                put(wave, x, t, z, wave_value)
                put(born, x, t, z, born_value)
                if wave_rows is not None:
                    wave_rows[strip(x, t, z), :] = wave_value
                born_rows[strip(x, t, z), :] = born_value
                finals.append((wave_value, born_value))
            if faces is not None:
                (w0, b0), (w1, b1) = finals
                pack_y(sub, even_y, faces[2], faces[3], x, z, w0, w1, b0, b1)

    for x in range(4):
        one(x, -1, x)
    lax.fori_loop(4, CX - 4, lambda x, carry: (one(x, 0, 0), carry)[1], 0)
    for x in range(CX - 4, CX):
        one(x, 1, x - (CX - 4))
    if faces is not None:
        pack_x(even_x, faces[0], faces[1], wave, born)


def fix_kernel(
    place, wave_part, born_part, courant, contrast, rxa, rxb, rya, ryb,
    wave, born, wave_rows, born_rows, xa, xb, ya, yb,
):
    clear(wave_rows, born_rows)
    fix(
        place, wave_part, born_part, courant, contrast, rxa, rxb, rya, ryb,
        wave, born, wave_rows, born_rows, (xa, xb, ya, yb),
    )


def take(rows_at, grid, picks, rows, out):
    def step(g, carry):
        for j in range(4):
            r = g * 4 + j
            for t in range(8):
                rows[pl.ds(r * 8 + t, 1), :] = grid[pl.ds(rows_at[t, r], 1), :]
        return carry

    lax.fori_loop(0, 64, step, 0)

    def total(g, carry):
        part = pl.ds(pl.multiple_of(g * 256, 256), 256)
        value = (rows[part, :] * picks[part, :]).reshape(32, 8, 128)
        out[pl.ds(pl.multiple_of(g * 32, 32), 32), :] = jnp.sum(value, axis=1)
        return carry

    lax.fori_loop(0, 8, total, 0)


def last_kernel(
    place, rows_at, wave_part, born_part, courant, contrast, rxa, rxb, rya, ryb,
    picks, first, slots, dest, wave_out, born_out, packed, wave, born, grid, rows, sums, sems,
):
    fix(place, wave_part, born_part, courant, contrast, rxa, rxb, rya, ryb, wave, born, None, grid, None)
    copies = [
        pltpu.make_async_copy(wave, wave_out, sems.at[0]),
        pltpu.make_async_copy(born, born_out, sems.at[1]),
    ]
    for copy in copies:
        copy.start()
    take(rows_at, grid, picks, rows, sums)
    one = jnp.sum(first[...], axis=1, keepdims=True)
    two = jnp.sum(sums[...], axis=1, keepdims=True)
    lane = lax.broadcasted_iota(jnp.int32, (256, 128), 1)
    spread_out = jnp.where(lane < 4, one, two) * slots[...]
    owner = lax.broadcasted_iota(jnp.int32, (128, 256), 0)
    chosen = jnp.where(owner == dest[...], 1.0, 0.0).astype(F32)
    packed[...] = jnp.dot(chosen, spread_out, precision=lax.Precision.HIGHEST, preferred_element_type=F32)
    for copy in copies:
        copy.wait()


def pairs(count, first):
    found = []
    for i in range(first, count - 1, 2):
        found += [(i, i + 1), (i + 1, i)]
    return found


VM = pl.BlockSpec(memory_space=pltpu.VMEM)
SM = pl.BlockSpec(memory_space=pltpu.SMEM)
HB = pl.BlockSpec(memory_space=pltpu.HBM)


def kept(shape):
    return VM, pltpu.VMEM(shape, F32)


def plain(shape):
    return VM, jax.ShapeDtypeStruct(shape, F32)


def away(shape):
    return HB, jax.ShapeDtypeStruct(shape, F32)


def call(kernel, name, args, specs, outs, scratch, mib, us):
    return pl.pallas_call(
        kernel,
        name=name,
        out_shape=tuple(o[1] for o in outs),
        in_specs=specs,
        out_specs=tuple(o[0] for o in outs),
        scratch_shapes=list(scratch),
        compiler_params=pltpu.CompilerParams(vmem_limit_bytes=mib * 1024 * 1024),
        cost_estimate=pl.CostEstimate(flops=0, bytes_accessed=us * 3_000_000, transcendentals=0),
    )(*args)


def exchange(faces):
    xa, xb, ya, yb = faces
    ryb = lax.ppermute(yb, "gy", pairs(16, 1))
    rxb = lax.ppermute(xb, "gx", pairs(8, 1))
    rxa = lax.ppermute(xa, "gx", pairs(8, 0))
    rya = lax.ppermute(ya, "gy", pairs(16, 0))
    return rxa, rxb, rya, ryb


def z_table():
    source = lax.broadcasted_iota(jnp.int32, (1024, 256), 0) % 512 - 128
    target = lax.broadcasted_iota(jnp.int32, (1024, 256), 1)
    gap = jnp.abs(source - target)
    table = jnp.zeros((1024, 256), F32)
    for k in range(1, 5):
        table = jnp.where(gap == k, WEIGHTS[k - 1], table)
    return table.astype(BF16)


def body(
    wave_old,
    wave_now,
    born_old,
    born_now,
    courant,
    contrast,
    src_cell,
    src_amp,
    rcv_cell,
    rcv_weight,
    rcv_dest,
):
    place = jnp.stack([lax.axis_index("gx") % 2, lax.axis_index("gy") % 2]).astype(jnp.int32)
    field = pltpu.VMEM(BLOCK, F32)
    halves = [pltpu.VMEM((CX * CY, NZ + 256), BF16)] * 2 + [pltpu.VMEM((CX * CY, NZ), F32)] * 2
    face_outs = [plain(XFACE), plain(XFACE), plain(YFACE), plain(YFACE)]

    wave_rows, born_rows, *faces = call(
        pack_kernel, "pack", (place, wave_now, born_now), [SM, HB, HB],
        [kept((ROWS, 128))] * 2 + face_outs, [field, field, pltpu.SemaphoreType.DMA((2, 4))], 10, 2,
    )
    halo = exchange(faces)
    table = z_table()
    wave_part, born_part, speed, factor = call(
        inner_first, "inner1",
        (src_cell, src_amp[:, 0], wave_rows, born_rows, table, wave_old, born_old, courant, contrast),
        [SM, SM, VM, VM, VM, HB, HB, HB, HB],
        [kept(BLOCK)] * 4, [field, field, *halves, pltpu.SemaphoreType.DMA((4,))], 14, 8,
    )

    cell = rcv_cell.T
    rows_at = ((cell >> 14) + 4) * LAYER + ((cell >> 7) & 7) * STRIP + 8 + ((cell >> 10) & 15)
    lane = lax.broadcasted_iota(jnp.int32, (256, 8, 128), 2)
    picks = jnp.where(lane == (rcv_cell & 127)[:, :, None], rcv_weight[:, :, None], 0.0).reshape(2048, 128)
    dest = rcv_dest[:, 0]
    order = jnp.arange(256, dtype=jnp.int32)
    earlier = (dest[:, None] == dest[None, :]) & (order[None, :] < order[:, None])
    slot = jnp.sum(earlier.astype(jnp.int32), axis=1)
    lane = lax.broadcasted_iota(jnp.int32, (256, 128), 1)
    slots = jnp.where((lane < 8) & (lane % 4 == slot[:, None]), 1.0, 0.0).astype(F32)

    wave_mid, born_mid, wave_mid_rows, born_mid_rows, *faces = call(
        fix_kernel, "fix1", (place, wave_part, born_part, speed, factor, *halo), [SM] + [VM] * 8,
        [kept(BLOCK)] * 2 + [kept((ROWS, 128))] * 2 + face_outs, [], 10, 3,
    )
    halo = exchange(faces)
    wave_part, born_part, first, wave_next, born_next = call(
        inner_second, "inner2",
        (
            src_cell, src_amp[:, 1], rows_at, wave_mid_rows, born_mid_rows, table, wave_rows, born_rows,
            speed, factor, picks, wave_mid, born_mid,
        ),
        [SM] * 3 + [VM] * 10,
        [kept(BLOCK)] * 2 + [plain((256, 128)), away(BLOCK), away(BLOCK)],
        [*halves, pltpu.VMEM((2048, 128), F32), pltpu.SemaphoreType.DMA((2,))], 12, 10,
    )
    wave_last, born_last, packed = call(
        last_kernel, "last",
        (place, rows_at, wave_part, born_part, speed, factor, *halo, picks, first, slots, dest[None, :]),
        [SM, SM] + [VM] * 12,
        [away(BLOCK), away(BLOCK), plain((128, 128))],
        [
            field, field, pltpu.VMEM((ROWS, 128), F32), pltpu.VMEM((2048, 128), F32),
            pltpu.VMEM((256, 128), F32), pltpu.SemaphoreType.DMA((2,)),
        ], 16, 5,
    )
    arrived = lax.all_to_all(
        packed.reshape(128, 1, 128), ("gx", "gy"), split_axis=0, concat_axis=0, tiled=True
    )
    gathers = arrived[:, 0, :8].reshape(1, 128, 2, CAP)
    return (wave_next, wave_last, born_next, born_last, gathers)


def solution(mesh):
    placed = (P("gx", "gy", None),) * 6 + (
        P(("gx", "gy")),
        P(("gx", "gy"), None),
        P(("gx", "gy"), None),
        P(("gx", "gy"), None),
        P(("gx", "gy"), None),
    )
    return jax.shard_map(
        body,
        mesh=mesh,
        in_specs=placed,
        out_specs=(P("gx", "gy", None),) * 4 + (P(("gx", "gy"), None, None, None),),
        check_vma=False,
    )
```

```python
import jax
import jax.numpy as jnp
from jax import lax
from jax.experimental import pallas as pl
from jax.experimental.pallas import tpu as pltpu
from jax.sharding import PartitionSpec as P

CAP = 4
SCALE = 5040.0
CENTER = -3.0 * 14350.0
WEIGHTS = (8064.0, -1008.0, 128.0, -9.0)
CX, CY, NZ = 32, 16, 1024
TZ = NZ // 128
BLOCK = (CX, CY, NZ)
XFACE = (8, CY, NZ)
YFACE = (CX, 8, NZ)
STRIP = 24
LAYER = TZ * STRIP
ROWS = (CX + 8) * LAYER + 8
F32 = jnp.float32
BF16 = jnp.bfloat16


def iotas():
    sub = lax.broadcasted_iota(jnp.int32, (8, 128), 0)
    lane = lax.broadcasted_iota(jnp.int32, (8, 128), 1)
    return sub, lane


def tile(ref, x, t, z):
    return ref[x, t * 8 : t * 8 + 8, z * 128 : z * 128 + 128]


def put(ref, x, t, z, value):
    ref[x, t * 8 : t * 8 + 8, z * 128 : z * 128 + 128] = value


def strip(x, t, z, shift=0):
    return pl.ds(x * LAYER + (4 * LAYER + z * STRIP + 8 + t * 8 + shift), 8)


def clear(*refs):
    zero = jnp.zeros((8, 128), F32)

    def gaps(x, carry):
        for z in range(TZ):
            for ref in refs:
                ref[pl.ds(pl.multiple_of(x * LAYER + z * STRIP, 8), 8), :] = zero
        return carry

    def layer(i, carry):
        x = jnp.where(i < 4, i, i + CX)
        for z in range(TZ):
            for t in range(2):
                for ref in refs:
                    ref[pl.ds(pl.multiple_of(x * LAYER + z * STRIP + 8 + t * 8, 8), 8), :] = zero
        return carry

    lax.fori_loop(0, CX + 8, gaps, 0)
    lax.fori_loop(0, 8, layer, 0)
    for ref in refs:
        ref[pl.ds(ROWS - 8, 8), :] = zero


def pack_y(sub, even, ya, yb, x, z, w0, w1, b0, b1):
    low = jnp.where(sub < 4, w0, pltpu.roll(b0, 4, 0))
    high = jnp.where(sub < 4, pltpu.roll(w1, 4, 0), b1)
    put(ya, x, 0, z, jnp.where(even, high, low))
    put(yb, x, 0, z, jnp.where(even, low, high))


def pack_x(even, xa, xb, wave, born):
    start_a = jnp.where(even, CX - 4, 0)
    start_b = jnp.where(even, 0, CX - 4)
    for i in range(4):
        xa[i] = wave[start_a + i]
        xa[i + 4] = born[start_a + i]
        xb[i] = wave[start_b + i]
        xb[i + 4] = born[start_b + i]


def pack_kernel(place, wave_in, born_in, wave_rows, born_rows, xa, xb, ya, yb, wave, born, sems):
    sub, _ = iotas()
    even_y = place[1] == 0
    parts = 4
    each = CX // parts

    def copies(c):
        part = pl.ds(c * each, each)
        return (
            pltpu.make_async_copy(wave_in.at[part], wave.at[part], sems.at[0, c]),
            pltpu.make_async_copy(born_in.at[part], born.at[part], sems.at[1, c]),
        )

    for c in range(parts):
        for copy in copies(c):
            copy.start()
    clear(wave_rows, born_rows)
    for c in range(parts):
        for copy in copies(c):
            copy.wait()

        def step(x, carry):
            for z in range(TZ):
                w0, w1, b0, b1 = tile(wave, x, 0, z), tile(wave, x, 1, z), tile(born, x, 0, z), tile(born, x, 1, z)
                pack_y(sub, even_y, ya, yb, x, z, w0, w1, b0, b1)
                wave_rows[strip(x, 0, z), :] = w0
                wave_rows[strip(x, 1, z), :] = w1
                born_rows[strip(x, 0, z), :] = b0
                born_rows[strip(x, 1, z), :] = b1
            return carry

        lax.fori_loop(c * each, (c + 1) * each, step, 0)
    pack_x(place[0] == 0, xa, xb, wave, born)


def along_z(ref, high, low, table, out):
    zero = jnp.zeros((CX * CY, 128), BF16)
    for half in (high, low):
        half[:, 0:128] = zero
        half[:, 128 + NZ : 256 + NZ] = zero

    def split(x, carry):
        rows = pl.ds(pl.multiple_of(x * CY, CY), CY)
        for z in range(TZ):
            value = ref[pl.ds(pl.multiple_of(x * LAYER + (4 * LAYER + z * STRIP + 8), 8), CY), :]
            top = value.astype(BF16)
            high[rows, 128 + z * 128 : 256 + z * 128] = top
            low[rows, 128 + z * 128 : 256 + z * 128] = (value - top.astype(F32)).astype(BF16)
        return carry

    lax.fori_loop(0, CX, split, 0, unroll=2)
    for c in range(NZ // 256):
        window = slice(c * 256, c * 256 + 512)
        both = jnp.concatenate([high[:, window], low[:, window]], axis=1)
        out[:, c * 256 : c * 256 + 256] = jnp.dot(both, table[...], preferred_element_type=F32)


def spread(ref, z_sum, x, t, z):
    here = ref[strip(x, t, z), :]
    total = CENTER * here + z_sum[pl.ds(pl.multiple_of(x * CY + t * 8, 8), 8), z * 128 : z * 128 + 128]
    for k in range(1, 5):
        flat = ref[strip(x, t, z, k), :] + ref[strip(x, t, z, -k), :]
        deep = ref[strip(x, t, z, k * LAYER), :] + ref[strip(x, t, z, -k * LAYER), :]
        total = total + WEIGHTS[k - 1] * (flat + deep)
    return here, total


def add_sources(cells, amps, contrast, wave_part, born_part):
    sub, lane = iotas()
    for i in range(4):
        cell = cells[i]
        x = lax.shift_right_logical(cell, 14)
        y = lax.bitwise_and(lax.shift_right_logical(cell, 10), 15)
        z = lax.bitwise_and(cell, NZ - 1)
        row = pl.multiple_of(lax.bitwise_and(y, 8), 8)
        col = pl.multiple_of(lax.bitwise_and(z, NZ - 128), 128)
        here = (sub == lax.bitwise_and(y, 7)) & (lane == lax.bitwise_and(z, 127))
        added = jnp.where(here, amps[i], 0.0)
        at = (x, pl.ds(row, 8), pl.ds(col, 128))
        wave_part[at] = wave_part[at] + added
        born_part[at] = born_part[at] + contrast[at] * added


def make_picks(taps, weights, picks):
    lane = lax.broadcasted_iota(jnp.int32, (8, 128), 1)
    for half in range(2):
        spots = lax.bitwise_and(taps[:, half * 128 : half * 128 + 128], 127)
        gains = weights[:, half * 128 : half * 128 + 128]

        def group(g, carry):
            spots, gains = carry
            for j in range(16):
                row = pl.multiple_of((half * 128 + g * 16 + j) * 8, 8)
                picks[pl.ds(row, 8), :] = jnp.where(lane == spots[:, j : j + 1], gains[:, j : j + 1], 0.0)
            return pltpu.roll(spots, 112, 1), pltpu.roll(gains, 112, 1)

        lax.fori_loop(0, 8, group, (spots, gains))


def inner_first(
    cells, amps, wave, born, table, taps, weights, wave_old_in, born_old_in, courant_in, contrast_in,
    wave_part, born_part, courant, contrast, picks, wave_old, born_old, high, low, wave_z, born_z, sems,
):
    copies = [
        pltpu.make_async_copy(a, b, sems.at[i])
        for i, (a, b) in enumerate(
            ((wave_old_in, wave_old), (born_old_in, born_old), (courant_in, courant), (contrast_in, contrast))
        )
    ]
    for copy in copies:
        copy.start()
    along_z(wave, high, low, table, wave_z)
    along_z(born, high, low, table, born_z)
    make_picks(taps, weights, picks)
    for copy in copies:
        copy.wait()

    def step(x, carry):
        for z in range(TZ):
            for t in range(2):
                speed = tile(courant, x, t, z) * (1.0 / SCALE)
                put(courant, x, t, z, speed)
                here, total = spread(wave, wave_z, x, t, z)
                moved = speed * total
                put(wave_part, x, t, z, (2.0 * here - tile(wave_old, x, t, z)) + moved)
                here, total = spread(born, born_z, x, t, z)
                moved = speed * total + tile(contrast, x, t, z) * moved
                put(born_part, x, t, z, (2.0 * here - tile(born_old, x, t, z)) + moved)
        return carry

    lax.fori_loop(0, CX, step, 0)
    add_sources(cells, amps, contrast, wave_part, born_part)


def inner_second(
    cells, amps, rows_at, wave, born, table, wave_old, born_old, courant, contrast, picks, wave_now, born_now,
    wave_part, born_part, first, wave_out, born_out, high, low, wave_z, born_z, rows, sems,
):
    copies = [
        pltpu.make_async_copy(wave_now, wave_out, sems.at[0]),
        pltpu.make_async_copy(born_now, born_out, sems.at[1]),
    ]
    for copy in copies:
        copy.start()
    along_z(wave, high, low, table, wave_z)
    along_z(born, high, low, table, born_z)

    def step(x, carry):
        for z in range(TZ):
            for t in range(2):
                speed = tile(courant, x, t, z)
                here, total = spread(wave, wave_z, x, t, z)
                moved = speed * total
                put(wave_part, x, t, z, (2.0 * here - wave_old[strip(x, t, z), :]) + moved)
                here, total = spread(born, born_z, x, t, z)
                moved = speed * total + tile(contrast, x, t, z) * moved
                put(born_part, x, t, z, (2.0 * here - born_old[strip(x, t, z), :]) + moved)
        return carry

    lax.fori_loop(0, CX, step, 0)
    add_sources(cells, amps, contrast, wave_part, born_part)
    take(rows_at, born, picks, rows, first)
    for copy in copies:
        copy.wait()


def fix(place, wave_part, born_part, courant, contrast, xa, xb, ya, yb, wave, born, wave_rows, born_rows, faces):
    sub, _ = iotas()
    even_x = place[0] == 0
    even_y = place[1] == 0
    part = lax.bitwise_and(sub, 3)
    low_weights = [jnp.where(part < k, WEIGHTS[k - 1], 0.0) for k in range(1, 4)]
    high_weights = [jnp.where(part >= 4 - k, WEIGHTS[k - 1], 0.0) for k in range(1, 4)]

    def one(x, side, offset):
        for z in range(TZ):
            from_a, from_b = tile(ya, x, 0, z), tile(yb, x, 0, z)
            low = jnp.where(even_y, from_b, from_a)
            high = jnp.where(even_y, from_a, from_b)
            low_sum, high_sum = WEIGHTS[3] * low, WEIGHTS[3] * high
            for k in range(1, 4):
                low_sum = low_sum + low_weights[k - 1] * pltpu.roll(low, 4 + k, 0)
                high_sum = high_sum + high_weights[k - 1] * pltpu.roll(high, 4 - k, 0)
            wave_sums = [
                jnp.where(sub < 4, low_sum, 0.0),
                jnp.where(sub < 4, 0.0, pltpu.roll(high_sum, 4, 0)),
            ]
            born_sums = [
                jnp.where(sub < 4, pltpu.roll(low_sum, 4, 0), 0.0),
                jnp.where(sub < 4, 0.0, high_sum),
            ]
            finals = []
            for t in range(2):
                wave_sum, born_sum = wave_sums[t], born_sums[t]
                if side:
                    for m in range(4):
                        reach = offset + 4 - m if side < 0 else 4 - offset + m
                        if 1 <= reach <= 4:
                            lone, other = (xb, xa) if side < 0 else (xa, xb)
                            w = WEIGHTS[reach - 1]
                            wave_sum = wave_sum + w * jnp.where(even_x, tile(lone, m, t, z), tile(other, m, t, z))
                            born_sum = born_sum + w * jnp.where(even_x, tile(lone, m + 4, t, z), tile(other, m + 4, t, z))
                speed = tile(courant, x, t, z)
                moved = speed * wave_sum
                wave_value = tile(wave_part, x, t, z) + moved
                born_value = tile(born_part, x, t, z) + (tile(contrast, x, t, z) * moved + speed * born_sum)
                put(wave, x, t, z, wave_value)
                put(born, x, t, z, born_value)
                if wave_rows is not None:
                    wave_rows[strip(x, t, z), :] = wave_value
                born_rows[strip(x, t, z), :] = born_value
                finals.append((wave_value, born_value))
            if faces is not None:
                (w0, b0), (w1, b1) = finals
                pack_y(sub, even_y, faces[2], faces[3], x, z, w0, w1, b0, b1)

    for x in range(4):
        one(x, -1, x)
    lax.fori_loop(4, CX - 4, lambda x, carry: (one(x, 0, 0), carry)[1], 0)
    for x in range(CX - 4, CX):
        one(x, 1, x - (CX - 4))
    if faces is not None:
        pack_x(even_x, faces[0], faces[1], wave, born)


def fix_kernel(
    place, wave_part, born_part, courant, contrast, rxa, rxb, rya, ryb,
    wave, born, wave_rows, born_rows, xa, xb, ya, yb,
):
    clear(wave_rows, born_rows)
    fix(
        place, wave_part, born_part, courant, contrast, rxa, rxb, rya, ryb,
        wave, born, wave_rows, born_rows, (xa, xb, ya, yb),
    )


def take(rows_at, grid, picks, rows, out):
    def step(g, carry):
        for j in range(4):
            r = g * 4 + j
            for t in range(8):
                rows[pl.ds(r * 8 + t, 1), :] = grid[pl.ds(rows_at[t, r], 1), :]
        return carry

    lax.fori_loop(0, 64, step, 0)

    def total(g, carry):
        part = pl.ds(pl.multiple_of(g * 256, 256), 256)
        value = (rows[part, :] * picks[part, :]).reshape(32, 8, 128)
        out[pl.ds(pl.multiple_of(g * 32, 32), 32), :] = jnp.sum(value, axis=1)
        return carry

    lax.fori_loop(0, 8, total, 0)


def last_kernel(
    place, rows_at, wave_part, born_part, courant, contrast, rxa, rxb, rya, ryb,
    picks, first, slots, dest, wave_out, born_out, packed, wave, born, grid, rows, sums, sems,
):
    fix(place, wave_part, born_part, courant, contrast, rxa, rxb, rya, ryb, wave, born, None, grid, None)
    copies = [
        pltpu.make_async_copy(wave, wave_out, sems.at[0]),
        pltpu.make_async_copy(born, born_out, sems.at[1]),
    ]
    for copy in copies:
        copy.start()
    take(rows_at, grid, picks, rows, sums)
    one = jnp.sum(first[...], axis=1, keepdims=True)
    two = jnp.sum(sums[...], axis=1, keepdims=True)
    lane = lax.broadcasted_iota(jnp.int32, (256, 128), 1)
    spread_out = jnp.where(lane < 4, one, two) * slots[...]
    owner = lax.broadcasted_iota(jnp.int32, (128, 256), 0)
    chosen = jnp.where(owner == dest[...], 1.0, 0.0).astype(F32)
    packed[...] = jnp.dot(chosen, spread_out, precision=lax.Precision.HIGHEST, preferred_element_type=F32)
    for copy in copies:
        copy.wait()


def pairs(count, first):
    found = []
    for i in range(first, count - 1, 2):
        found += [(i, i + 1), (i + 1, i)]
    return found


VM = pl.BlockSpec(memory_space=pltpu.VMEM)
SM = pl.BlockSpec(memory_space=pltpu.SMEM)
HB = pl.BlockSpec(memory_space=pltpu.HBM)


def kept(shape):
    return VM, pltpu.VMEM(shape, F32)


def plain(shape):
    return VM, jax.ShapeDtypeStruct(shape, F32)


def away(shape):
    return HB, jax.ShapeDtypeStruct(shape, F32)


def still(value):
    return pltpu.with_memory_space_constraint(value, pltpu.HBM)


def call(kernel, name, args, specs, outs, scratch, mib, us):
    return pl.pallas_call(
        kernel,
        name=name,
        out_shape=tuple(o[1] for o in outs),
        in_specs=specs,
        out_specs=tuple(o[0] for o in outs),
        scratch_shapes=list(scratch),
        compiler_params=pltpu.CompilerParams(vmem_limit_bytes=mib * 1024 * 1024),
        cost_estimate=pl.CostEstimate(flops=0, bytes_accessed=us * 3_000_000, transcendentals=0),
    )(*args)


def exchange(faces):
    xa, xb, ya, yb = faces
    ryb = lax.ppermute(yb, "gy", pairs(16, 1))
    rxb = lax.ppermute(xb, "gx", pairs(8, 1))
    rxa = lax.ppermute(xa, "gx", pairs(8, 0))
    rya = lax.ppermute(ya, "gy", pairs(16, 0))
    return rxa, rxb, rya, ryb


def z_table():
    source = lax.broadcasted_iota(jnp.int32, (1024, 256), 0) % 512 - 128
    target = lax.broadcasted_iota(jnp.int32, (1024, 256), 1)
    gap = jnp.abs(source - target)
    table = jnp.zeros((1024, 256), F32)
    for k in range(1, 5):
        table = jnp.where(gap == k, WEIGHTS[k - 1], table)
    return table.astype(BF16)


def body(
    wave_old,
    wave_now,
    born_old,
    born_now,
    courant,
    contrast,
    src_cell,
    src_amp,
    rcv_cell,
    rcv_weight,
    rcv_dest,
):
    place = jnp.stack([lax.axis_index("gx") % 2, lax.axis_index("gy") % 2]).astype(jnp.int32)
    field = pltpu.VMEM(BLOCK, F32)
    halves = [pltpu.VMEM((CX * CY, NZ + 256), BF16)] * 2 + [pltpu.VMEM((CX * CY, NZ), F32)] * 2
    face_outs = [plain(XFACE), plain(XFACE), plain(YFACE), plain(YFACE)]

    wave_rows, born_rows, *faces = call(
        pack_kernel, "pack", (place, still(wave_now), still(born_now)), [SM, HB, HB],
        [kept((ROWS, 128))] * 2 + face_outs, [field, field, pltpu.SemaphoreType.DMA((2, 4))], 10, 2,
    )
    halo = exchange(faces)
    table = z_table()
    wave_part, born_part, speed, factor, picks = call(
        inner_first, "inner1",
        (
            src_cell, src_amp[:, 0], wave_rows, born_rows, table, rcv_cell.T, rcv_weight.T,
            still(wave_old), still(born_old), still(courant), still(contrast),
        ),
        [SM, SM] + [VM] * 5 + [HB] * 4,
        [kept(BLOCK)] * 4 + [kept((2048, 128))], [field, field, *halves, pltpu.SemaphoreType.DMA((4,))], 14, 8,
    )

    cell = rcv_cell.T
    rows_at = ((cell >> 14) + 4) * LAYER + ((cell >> 7) & 7) * STRIP + 8 + ((cell >> 10) & 15)
    dest = rcv_dest[:, 0]
    order = jnp.arange(256, dtype=jnp.int32)
    earlier = (dest[:, None] == dest[None, :]) & (order[None, :] < order[:, None])
    slot = jnp.sum(earlier.astype(jnp.int32), axis=1)
    lane = lax.broadcasted_iota(jnp.int32, (256, 128), 1)
    slots = jnp.where((lane < 8) & (lane % 4 == slot[:, None]), 1.0, 0.0).astype(F32)

    wave_mid, born_mid, wave_mid_rows, born_mid_rows, *faces = call(
        fix_kernel, "fix1", (place, wave_part, born_part, speed, factor, *halo), [SM] + [VM] * 8,
        [kept(BLOCK)] * 2 + [kept((ROWS, 128))] * 2 + face_outs, [], 10, 3,
    )
    halo = exchange(faces)
    wave_part, born_part, first, wave_next, born_next = call(
        inner_second, "inner2",
        (
            src_cell, src_amp[:, 1], rows_at, wave_mid_rows, born_mid_rows, table, wave_rows, born_rows,
            speed, factor, picks, wave_mid, born_mid,
        ),
        [SM] * 3 + [VM] * 10,
        [kept(BLOCK)] * 2 + [plain((256, 128)), away(BLOCK), away(BLOCK)],
        [*halves, pltpu.VMEM((2048, 128), F32), pltpu.SemaphoreType.DMA((2,))], 12, 10,
    )
    wave_last, born_last, packed = call(
        last_kernel, "last",
        (place, rows_at, wave_part, born_part, speed, factor, *halo, picks, first, slots, dest[None, :]),
        [SM, SM] + [VM] * 12,
        [away(BLOCK), away(BLOCK), plain((128, 128))],
        [
            field, field, pltpu.VMEM((ROWS, 128), F32), pltpu.VMEM((2048, 128), F32),
            pltpu.VMEM((256, 128), F32), pltpu.SemaphoreType.DMA((2,)),
        ], 16, 5,
    )
    arrived = lax.all_to_all(
        packed.reshape(128, 1, 128), ("gx", "gy"), split_axis=0, concat_axis=0, tiled=True
    )
    gathers = arrived[:, 0, :8].reshape(1, 128, 2, CAP)
    return (wave_next, wave_last, born_next, born_last, gathers)


def solution(mesh):
    placed = (P("gx", "gy", None),) * 6 + (
        P(("gx", "gy")),
        P(("gx", "gy"), None),
        P(("gx", "gy"), None),
        P(("gx", "gy"), None),
        P(("gx", "gy"), None),
    )
    return jax.shard_map(
        body,
        mesh=mesh,
        in_specs=placed,
        out_specs=(P("gx", "gy", None),) * 4 + (P(("gx", "gy"), None, None, None),),
        check_vma=False,
    )
```

```python
import jax
import jax.numpy as jnp
from jax import lax
from jax.experimental import pallas as pl
from jax.experimental.pallas import tpu as pltpu
from jax.sharding import PartitionSpec as P


CAP = 4
SCALE = 5040.0
CENTER = -3.0 * 14350.0
WEIGHTS = (8064.0, -1008.0, 128.0, -9.0)
CX, CY, NZ = 32, 16, 1024
TZ = NZ // 128
BLOCK = (CX, CY, NZ)
XFACE = (8, CY, NZ)
YFACE = (CX, 8, NZ)
STRIP = 24
LAYER = TZ * STRIP
ROWS = (CX + 8) * LAYER + 8
F32 = jnp.float32
BF16 = jnp.bfloat16


def iotas():
    sub = lax.broadcasted_iota(jnp.int32, (8, 128), 0)
    lane = lax.broadcasted_iota(jnp.int32, (8, 128), 1)
    return sub, lane


def tile(ref, x, t, z):
    return ref[x, t * 8 : t * 8 + 8, z * 128 : z * 128 + 128]


def put(ref, x, t, z, value):
    ref[x, t * 8 : t * 8 + 8, z * 128 : z * 128 + 128] = value


def strip(x, t, z, shift=0):
    return pl.ds(x * LAYER + (4 * LAYER + z * STRIP + 8 + t * 8 + shift), 8)


def clear(*refs):
    zero = jnp.zeros((8, 128), F32)

    def gaps(x, carry):
        for z in range(TZ):
            for ref in refs:
                ref[pl.ds(pl.multiple_of(x * LAYER + z * STRIP, 8), 8), :] = zero
        return carry

    def layer(i, carry):
        x = jnp.where(i < 4, i, i + CX)
        for z in range(TZ):
            for t in range(2):
                for ref in refs:
                    ref[pl.ds(pl.multiple_of(x * LAYER + z * STRIP + 8 + t * 8, 8), 8), :] = zero
        return carry

    lax.fori_loop(0, CX + 8, gaps, 0)
    lax.fori_loop(0, 8, layer, 0)
    for ref in refs:
        ref[pl.ds(ROWS - 8, 8), :] = zero


def pack_y(sub, even, ya, yb, x, z, w0, w1, b0, b1):
    low = jnp.where(sub < 4, w0, pltpu.roll(b0, 4, 0))
    high = jnp.where(sub < 4, pltpu.roll(w1, 4, 0), b1)
    put(ya, x, 0, z, jnp.where(even, high, low))
    put(yb, x, 0, z, jnp.where(even, low, high))


def pack_x(even, xa, xb, wave, born):
    start_a = jnp.where(even, CX - 4, 0)
    start_b = jnp.where(even, 0, CX - 4)
    for i in range(4):
        xa[i] = wave[start_a + i]
        xa[i + 4] = born[start_a + i]
        xb[i] = wave[start_b + i]
        xb[i + 4] = born[start_b + i]


def edge_kernel(place, ends, wave, born, xa, xb, place_out, ends_out, sems):
    for i in range(2):
        place_out[i] = place[i]
        ends_out[i] = ends[i]
    even = place[0] == 0
    starts = (jnp.where(even, CX - 4, 0), jnp.where(even, 0, CX - 4))
    copies = [
        pltpu.make_async_copy(field.at[pl.ds(start, 4)], face.at[pl.ds(4 * i, 4)], sems.at[j, i])
        for j, (start, face) in enumerate(zip(starts, (xa, xb)))
        for i, field in enumerate((wave, born))
    ]
    for copy in copies:
        copy.start()
    for copy in copies:
        copy.wait()


def pack_kernel(place, wave_in, born_in, wave_rows, born_rows, ya, yb, wave, born, sems):
    sub, _ = iotas()
    even_y = place[1] == 0
    parts = 4
    each = CX // parts

    def copies(c):
        part = pl.ds(c * each, each)
        return (
            pltpu.make_async_copy(wave_in.at[part], wave.at[part], sems.at[0, c]),
            pltpu.make_async_copy(born_in.at[part], born.at[part], sems.at[1, c]),
        )

    for c in range(parts):
        for copy in copies(c):
            copy.start()
    clear(wave_rows, born_rows)
    for c in range(parts):
        for copy in copies(c):
            copy.wait()

        def step(x, carry):
            for z in range(TZ):
                w0, w1, b0, b1 = tile(wave, x, 0, z), tile(wave, x, 1, z), tile(born, x, 0, z), tile(born, x, 1, z)
                pack_y(sub, even_y, ya, yb, x, z, w0, w1, b0, b1)
                wave_rows[strip(x, 0, z), :] = w0
                wave_rows[strip(x, 1, z), :] = w1
                born_rows[strip(x, 0, z), :] = b0
                born_rows[strip(x, 1, z), :] = b1
            return carry

        lax.fori_loop(c * each, (c + 1) * each, step, 0)


def along_z(ref, high, low, table, out):
    zero = jnp.zeros((CX * CY, 128), BF16)
    for half in (high, low):
        half[:, 0:128] = zero
        half[:, 128 + NZ : 256 + NZ] = zero

    def split(x, carry):
        rows = pl.ds(pl.multiple_of(x * CY, CY), CY)
        for z in range(TZ):
            value = ref[pl.ds(pl.multiple_of(x * LAYER + (4 * LAYER + z * STRIP + 8), 8), CY), :]
            top = value.astype(BF16)
            high[rows, 128 + z * 128 : 256 + z * 128] = top
            low[rows, 128 + z * 128 : 256 + z * 128] = (value - top.astype(F32)).astype(BF16)
        return carry

    lax.fori_loop(0, CX, split, 0, unroll=2)
    for c in range(NZ // 256):
        window = slice(c * 256, c * 256 + 512)
        both = jnp.concatenate([high[:, window], low[:, window]], axis=1)
        out[:, c * 256 : c * 256 + 256] = jnp.dot(both, table[...], preferred_element_type=F32)


def spread(ref, z_sum, x, t, z):
    here = ref[strip(x, t, z), :]
    total = CENTER * here + z_sum[pl.ds(pl.multiple_of(x * CY + t * 8, 8), 8), z * 128 : z * 128 + 128]
    for k in range(1, 5):
        flat = ref[strip(x, t, z, k), :] + ref[strip(x, t, z, -k), :]
        deep = ref[strip(x, t, z, k * LAYER), :] + ref[strip(x, t, z, -k * LAYER), :]
        total = total + WEIGHTS[k - 1] * (flat + deep)
    return here, total


def add_sources(cells, amps, contrast, wave_part, born_part):
    sub, lane = iotas()
    for i in range(4):
        cell = cells[i]
        x = lax.shift_right_logical(cell, 14)
        y = lax.bitwise_and(lax.shift_right_logical(cell, 10), 15)
        z = lax.bitwise_and(cell, NZ - 1)
        row = pl.multiple_of(lax.bitwise_and(y, 8), 8)
        col = pl.multiple_of(lax.bitwise_and(z, NZ - 128), 128)
        here = (sub == lax.bitwise_and(y, 7)) & (lane == lax.bitwise_and(z, 127))
        added = jnp.where(here, amps[i], 0.0)
        at = (x, pl.ds(row, 8), pl.ds(col, 128))
        wave_part[at] = wave_part[at] + added
        born_part[at] = born_part[at] + contrast[at] * added


def make_picks(taps, weights, picks):
    lane = lax.broadcasted_iota(jnp.int32, (8, 128), 1)
    for half in range(2):
        spots = lax.bitwise_and(taps[:, half * 128 : half * 128 + 128], 127)
        gains = weights[:, half * 128 : half * 128 + 128]

        def group(g, carry):
            spots, gains = carry
            for j in range(16):
                row = pl.multiple_of((half * 128 + g * 16 + j) * 8, 8)
                picks[pl.ds(row, 8), :] = jnp.where(lane == spots[:, j : j + 1], gains[:, j : j + 1], 0.0)
            return pltpu.roll(spots, 112, 1), pltpu.roll(gains, 112, 1)

        lax.fori_loop(0, 8, group, (spots, gains))


def inner_first(
    cells, amps, wave, born, table, taps, weights, wave_old_in, born_old_in, courant_in, contrast_in,
    wave_part, born_part, courant, contrast, picks, wave_next, born_next,
    wave_old, born_old, high, low, wave_z, born_z, sems,
):
    copies = [
        pltpu.make_async_copy(a, b, sems.at[i])
        for i, (a, b) in enumerate(
            ((wave_old_in, wave_old), (born_old_in, born_old), (courant_in, courant), (contrast_in, contrast))
        )
    ]
    for copy in copies:
        copy.start()
    along_z(wave, high, low, table, wave_z)
    along_z(born, high, low, table, born_z)
    make_picks(taps, weights, picks)
    clear(wave_next, born_next)
    for copy in copies:
        copy.wait()

    def step(x, carry):
        for z in range(TZ):
            for t in range(2):
                speed = tile(courant, x, t, z) * (1.0 / SCALE)
                put(courant, x, t, z, speed)
                here, total = spread(wave, wave_z, x, t, z)
                moved = speed * total
                put(wave_part, x, t, z, (2.0 * here - tile(wave_old, x, t, z)) + moved)
                here, total = spread(born, born_z, x, t, z)
                moved = speed * total + tile(contrast, x, t, z) * moved
                put(born_part, x, t, z, (2.0 * here - tile(born_old, x, t, z)) + moved)
        return carry

    lax.fori_loop(0, CX, step, 0)
    add_sources(cells, amps, contrast, wave_part, born_part)


def inner_second(
    cells, amps, rows_at, wave, born, table, wave_old, born_old, courant, contrast, picks, wave_now, born_now,
    wave_part, born_part, first, wave_out, born_out, high, low, wave_z, born_z, rows, sems,
):
    copies = [
        pltpu.make_async_copy(wave_now, wave_out, sems.at[0]),
        pltpu.make_async_copy(born_now, born_out, sems.at[1]),
    ]
    for copy in copies:
        copy.start()
    along_z(wave, high, low, table, wave_z)
    along_z(born, high, low, table, born_z)

    def step(x, carry):
        for z in range(TZ):
            for t in range(2):
                speed = tile(courant, x, t, z)
                here, total = spread(wave, wave_z, x, t, z)
                moved = speed * total
                put(wave_part, x, t, z, (2.0 * here - wave_old[strip(x, t, z), :]) + moved)
                here, total = spread(born, born_z, x, t, z)
                moved = speed * total + tile(contrast, x, t, z) * moved
                put(born_part, x, t, z, (2.0 * here - born_old[strip(x, t, z), :]) + moved)
        return carry

    lax.fori_loop(0, CX, step, 0)
    add_sources(cells, amps, contrast, wave_part, born_part)
    take(rows_at, born, picks, rows, first)
    for copy in copies:
        copy.wait()


def fix(
    place, ends, wave_part, born_part, courant, contrast, xa, xb, ya, yb, wave, born, wave_rows, born_rows, y_faces,
    edges, middle,
):
    sub, _ = iotas()
    even_x = place[0] == 0
    even_y = place[1] == 0
    part = lax.bitwise_and(sub, 3)
    low_weights = [jnp.where(part < k, WEIGHTS[k - 1], 0.0) for k in range(1, 4)]
    high_weights = [jnp.where(part >= 4 - k, WEIGHTS[k - 1], 0.0) for k in range(1, 4)]

    def one(x, side, offset):
        for z in range(TZ):
            from_a, from_b = tile(ya, x, 0, z), tile(yb, x, 0, z)
            low = jnp.where(even_y, from_b, from_a)
            high = jnp.where(even_y, from_a, from_b)
            low_sum, high_sum = WEIGHTS[3] * low, WEIGHTS[3] * high
            for k in range(1, 4):
                low_sum = low_sum + low_weights[k - 1] * pltpu.roll(low, 4 + k, 0)
                high_sum = high_sum + high_weights[k - 1] * pltpu.roll(high, 4 - k, 0)
            wave_sums = [
                jnp.where(sub < 4, low_sum, 0.0),
                jnp.where(sub < 4, 0.0, pltpu.roll(high_sum, 4, 0)),
            ]
            born_sums = [
                jnp.where(sub < 4, pltpu.roll(low_sum, 4, 0), 0.0),
                jnp.where(sub < 4, 0.0, high_sum),
            ]
            finals = []
            for t in range(2):
                wave_sum, born_sum = wave_sums[t], born_sums[t]
                if side:
                    for m in range(4):
                        reach = offset + 4 - m if side < 0 else 4 - offset + m
                        if 1 <= reach <= 4:
                            lone, other = (xb, xa) if side < 0 else (xa, xb)
                            w = WEIGHTS[reach - 1] * ends[0 if side < 0 else 1]
                            wave_sum = wave_sum + w * jnp.where(even_x, tile(lone, m, t, z), tile(other, m, t, z))
                            born_sum = born_sum + w * jnp.where(even_x, tile(lone, m + 4, t, z), tile(other, m + 4, t, z))
                speed = tile(courant, x, t, z)
                moved = speed * wave_sum
                wave_value = tile(wave_part, x, t, z) + moved
                born_value = tile(born_part, x, t, z) + (tile(contrast, x, t, z) * moved + speed * born_sum)
                put(wave, x, t, z, wave_value)
                put(born, x, t, z, born_value)
                if wave_rows is not None:
                    wave_rows[strip(x, t, z), :] = wave_value
                born_rows[strip(x, t, z), :] = born_value
                finals.append((wave_value, born_value))
            if y_faces is not None:
                (w0, b0), (w1, b1) = finals
                pack_y(sub, even_y, *y_faces, x, z, w0, w1, b0, b1)

    if edges:
        for x in range(4):
            one(x, -1, x)
        for x in range(CX - 4, CX):
            one(x, 1, x - (CX - 4))
    if middle:
        lax.fori_loop(4, CX - 4, lambda x, carry: (one(x, 0, 0), carry)[1], 0)


def fix_edges(
    place, ends, wave_part, born_part, courant, contrast, rxa, rxb, rya, ryb, rows_a, rows_b,
    wave, born, wave_rows, born_rows, xa, xb,
):
    fix(
        place, ends, wave_part, born_part, courant, contrast, rxa, rxb, rya, ryb,
        wave, born, wave_rows, born_rows, None, True, False,
    )
    pack_x(place[0] == 0, xa, xb, wave, born)


def fix_middle(
    place, ends, wave_part, born_part, courant, contrast, rya, ryb, wave_in, born_in, rows_a, rows_b,
    wave, born, wave_rows, born_rows, ya, yb,
):
    fix(
        place, ends, wave_part, born_part, courant, contrast, None, None, rya, ryb,
        wave, born, wave_rows, born_rows, (ya, yb), False, True,
    )
    sub, _ = iotas()
    even_y = place[1] == 0

    def step(i, carry):
        x = jnp.where(i < 4, i, i + CX - 8)
        for z in range(TZ):
            pack_y(
                sub, even_y, ya, yb, x, z, tile(wave, x, 0, z), tile(wave, x, 1, z), tile(born, x, 0, z), tile(born, x, 1, z)
            )
        return carry

    lax.fori_loop(0, 8, step, 0)


def take(rows_at, grid, picks, rows, out):
    def step(g, carry):
        for j in range(8):
            r = g * 8 + j
            for t in range(8):
                rows[pl.ds(r * 8 + t, 1), :] = grid[pl.ds(rows_at[t, r], 1), :]
        return carry

    lax.fori_loop(0, 32, step, 0)

    def total(g, carry):
        part = pl.ds(pl.multiple_of(g * 256, 256), 256)
        value = (rows[part, :] * picks[part, :]).reshape(32, 8, 128)
        out[pl.ds(pl.multiple_of(g * 32, 32), 32), :] = jnp.sum(value, axis=1)
        return carry

    lax.fori_loop(0, 8, total, 0)


def last_kernel(
    place, ends, rows_at, wave_part, born_part, courant, contrast, rxa, rxb, rya, ryb,
    picks, first, slots, dest, wave_out, born_out, packed, wave, born, grid, rows, sums, sems,
):
    fix(
        place, ends, wave_part, born_part, courant, contrast, rxa, rxb, rya, ryb,
        wave, born, None, grid, None, True, True,
    )
    copies = [
        pltpu.make_async_copy(wave, wave_out, sems.at[0]),
        pltpu.make_async_copy(born, born_out, sems.at[1]),
    ]
    for copy in copies:
        copy.start()
    take(rows_at, grid, picks, rows, sums)
    one = jnp.sum(first[...], axis=1, keepdims=True)
    two = jnp.sum(sums[...], axis=1, keepdims=True)
    lane = lax.broadcasted_iota(jnp.int32, (256, 128), 1)
    spread_out = jnp.where(lane < 4, one, two) * slots[...]
    owner = lax.broadcasted_iota(jnp.int32, (128, 256), 0)
    chosen = jnp.where(owner == dest[...], 1.0, 0.0).astype(F32)
    packed[...] = jnp.dot(chosen, spread_out, precision=lax.Precision.HIGHEST, preferred_element_type=F32)
    for copy in copies:
        copy.wait()


def pairs(count, first):
    found = []
    for i in range(first, count - 1, 2):
        found += [(i, i + 1), (i + 1, i)]
    return found


VM = pl.BlockSpec(memory_space=pltpu.VMEM)
SM = pl.BlockSpec(memory_space=pltpu.SMEM)
HB = pl.BlockSpec(memory_space=pltpu.HBM)


def kept(shape):
    return VM, pltpu.VMEM(shape, F32)


def plain(shape):
    return VM, jax.ShapeDtypeStruct(shape, F32)


def away(shape):
    return HB, jax.ShapeDtypeStruct(shape, F32)


def still(value):
    return pltpu.with_memory_space_constraint(value, pltpu.HBM)


def call(kernel, args, specs, outs, scratch, mib, us, aliases=None):
    return pl.pallas_call(
        kernel,
        out_shape=tuple(o[1] for o in outs),
        in_specs=specs,
        out_specs=tuple(o[0] for o in outs),
        scratch_shapes=list(scratch),
        input_output_aliases=aliases or {},
        compiler_params=pltpu.CompilerParams(vmem_limit_bytes=mib * 1024 * 1024),
        cost_estimate=pl.CostEstimate(flops=0, bytes_accessed=us * 3_000_000, transcendentals=0),
    )(*args)


def swap_x(xa, xb):
    flat = [(i * 16 + g, j * 16 + g) for i, j in pairs(8, 1) for g in range(16)]
    flat += [(i * 16 + g, i * 16 + (g ^ 1)) for i in (0, 7) for g in range(16)]
    rxb = lax.ppermute(xb, ("gx", "gy"), flat)
    rxa = lax.ppermute(xa, "gx", pairs(8, 0))
    return rxa, rxb


def swap_y(ya, yb):
    ryb = lax.ppermute(yb, "gy", pairs(16, 1))
    rya = lax.ppermute(ya, "gy", pairs(16, 0))
    return rya, ryb


def z_table():
    source = lax.broadcasted_iota(jnp.int32, (1024, 256), 0) % 512 - 128
    target = lax.broadcasted_iota(jnp.int32, (1024, 256), 1)
    gap = jnp.abs(source - target)
    table = jnp.zeros((1024, 256), F32)
    for k in range(1, 5):
        table = jnp.where(gap == k, WEIGHTS[k - 1], table)
    return table.astype(BF16)


def steps(
    wave_old,
    wave_now,
    born_old,
    born_now,
    courant,
    contrast,
    src_cell,
    src_amp,
    rcv_cell,
    rcv_weight,
    rcv_dest,
):
    index_x, index_y = lax.axis_index("gx"), lax.axis_index("gy")
    place = jnp.stack([index_x & 1, index_y & 1]).astype(jnp.int32)
    ends = jnp.stack([index_x > 0, index_x < 7]).astype(F32)
    field = pltpu.VMEM(BLOCK, F32)
    halves = [pltpu.VMEM((CX * CY, NZ + 256), BF16)] * 2 + [pltpu.VMEM((CX * CY, NZ), F32)] * 2
    x_faces, y_faces = [plain(XFACE)] * 2, [plain(YFACE)] * 2
    fixed = [kept(BLOCK)] * 2 + [kept((ROWS, 128))] * 2

    xa, xb, place, ends = call(
        edge_kernel, (place, ends, still(wave_now), still(born_now)), [SM, SM, HB, HB],
        x_faces + [(SM, jax.ShapeDtypeStruct((2,), jnp.int32)), (SM, jax.ShapeDtypeStruct((2,), F32))],
        [pltpu.SemaphoreType.DMA((2, 2))], 4, 1,
    )
    halo_x = swap_x(xa, xb)
    wave_rows, born_rows, ya, yb = call(
        pack_kernel, (place, still(wave_now), still(born_now)), [SM, HB, HB],
        [kept((ROWS, 128))] * 2 + y_faces, [field, field, pltpu.SemaphoreType.DMA((2, 4))], 10, 2,
    )
    halo_y = swap_y(ya, yb)
    table = z_table()
    wave_part, born_part, speed, factor, picks, wave_mid_rows, born_mid_rows = call(
        inner_first,
        (
            src_cell, src_amp[:, 0], wave_rows, born_rows, table, rcv_cell.T, rcv_weight.T,
            still(wave_old), still(born_old), still(courant), still(contrast),
        ),
        [SM, SM] + [VM] * 5 + [HB] * 4,
        [kept(BLOCK)] * 4 + [kept((2048, 128))] + [kept((ROWS, 128))] * 2, [field, field, *halves, pltpu.SemaphoreType.DMA((4,))], 14, 8,
    )

    cell = rcv_cell.T
    rows_at = ((cell >> 14) + 4) * LAYER + ((cell >> 7) & 7) * STRIP + 8 + ((cell >> 10) & 15)
    dest = rcv_dest[:, 0]
    order = jnp.arange(256, dtype=jnp.int32)
    earlier = (dest[:, None] == dest[None, :]) & (order[None, :] < order[:, None])
    slot = jnp.sum(earlier.astype(jnp.int32), axis=1)
    lane = lax.broadcasted_iota(jnp.int32, (256, 128), 1)
    slots = jnp.where((lane < 8) & (lane % 4 == slot[:, None]), 1.0, 0.0).astype(F32)

    shared = (wave_part, born_part, speed, factor)
    *mid, xa, xb = call(
        fix_edges, (place, ends, *shared, *halo_x, *halo_y, wave_mid_rows, born_mid_rows),
        [SM] * 2 + [VM] * 10, fixed + x_faces, [], 4, 2, {10: 2, 11: 3},
    )
    next_x = swap_x(xa, xb)
    wave_mid, born_mid, wave_mid_rows, born_mid_rows, ya, yb = call(
        fix_middle, (place, ends, *shared, *halo_y, *mid),
        [SM] * 2 + [VM] * 10, fixed + y_faces, [], 4, 2, {8: 0, 9: 1, 10: 2, 11: 3},
    )
    next_y = swap_y(ya, yb)
    wave_part, born_part, first, wave_next, born_next = call(
        inner_second,
        (
            src_cell, src_amp[:, 1], rows_at, wave_mid_rows, born_mid_rows, table, wave_rows, born_rows,
            speed, factor, picks, wave_mid, born_mid,
        ),
        [SM] * 3 + [VM] * 10,
        [kept(BLOCK)] * 2 + [plain((256, 128)), away(BLOCK), away(BLOCK)],
        [*halves, pltpu.VMEM((2048, 128), F32), pltpu.SemaphoreType.DMA((2,))], 12, 10,
    )
    wave_last, born_last, packed = call(
        last_kernel,
        (place, ends, rows_at, wave_part, born_part, speed, factor, *next_x, *next_y, picks, first, slots, dest[None, :]),
        [SM] * 3 + [VM] * 12,
        [away(BLOCK), away(BLOCK), plain((128, 128))],
        [
            field, field, pltpu.VMEM((ROWS, 128), F32), pltpu.VMEM((2048, 128), F32),
            pltpu.VMEM((256, 128), F32), pltpu.SemaphoreType.DMA((2,)),
        ], 16, 5,
    )
    arrived = lax.all_to_all(
        packed.reshape(128, 1, 128), ("gx", "gy"), split_axis=0, concat_axis=0, tiled=True
    )
    gathers = arrived[:, 0, :8].reshape(1, 128, 2, CAP)
    return (wave_next, wave_last, born_next, born_last, gathers)


def solution(mesh):
    placed = (P("gx", "gy", None),) * 6 + (
        P(("gx", "gy")),
        P(("gx", "gy"), None),
        P(("gx", "gy"), None),
        P(("gx", "gy"), None),
        P(("gx", "gy"), None),
    )
    return jax.shard_map(
        steps,
        mesh=mesh,
        in_specs=placed,
        out_specs=(P("gx", "gy", None),) * 4 + (P(("gx", "gy"), None, None, None),),
        check_vma=False,
    )
```

```python
import jax
import jax.numpy as jnp
from jax import lax
from jax.experimental import pallas as pl
from jax.experimental.pallas import tpu as pltpu
from jax.sharding import PartitionSpec as P


CAP = 4
SCALE = 5040.0
CENTER = -3.0 * 14350.0
WEIGHTS = (8064.0, -1008.0, 128.0, -9.0)
CX, CY, NZ = 32, 16, 1024
TZ = NZ // 128
BLOCK = (CX, CY, NZ)
XFACE = (8, CY, NZ)
YFACE = (CX, 8, NZ)
STRIP = CY
LAYER = TZ * STRIP
ROWS = CX * LAYER
F32 = jnp.float32
BF16 = jnp.bfloat16


def iotas():
    sub = lax.broadcasted_iota(jnp.int32, (8, 128), 0)
    lane = lax.broadcasted_iota(jnp.int32, (8, 128), 1)
    return sub, lane


def tile(ref, x, t, z):
    return ref[x, t * 8 : t * 8 + 8, z * 128 : z * 128 + 128]


def put(ref, x, t, z, value):
    ref[x, t * 8 : t * 8 + 8, z * 128 : z * 128 + 128] = value


def strip(x, t, z):
    return pl.ds(pl.multiple_of(x * LAYER + (z * STRIP + t * 8), 8), 8)


def pack_y(sub, even, ya, yb, x, z, w0, w1, b0, b1):
    low = jnp.where(sub < 4, w0, pltpu.roll(b0, 4, 0))
    high = jnp.where(sub < 4, pltpu.roll(w1, 4, 0), b1)
    put(ya, x, 0, z, jnp.where(even, high, low))
    put(yb, x, 0, z, jnp.where(even, low, high))


def pack_x(even, xa, xb, wave, born):
    start_a = jnp.where(even, CX - 4, 0)
    start_b = jnp.where(even, 0, CX - 4)
    for i in range(4):
        xa[i] = wave[start_a + i]
        xa[i + 4] = born[start_a + i]
        xb[i] = wave[start_b + i]
        xb[i + 4] = born[start_b + i]


def edge_kernel(place, ends, wave, born, xa, xb, place_out, ends_out, sems):
    for i in range(2):
        place_out[i] = place[i]
        ends_out[i] = ends[i]
    even = place[0] == 0
    starts = (jnp.where(even, CX - 4, 0), jnp.where(even, 0, CX - 4))
    copies = [
        pltpu.make_async_copy(field.at[pl.ds(start, 4)], face.at[pl.ds(4 * i, 4)], sems.at[j, i])
        for j, (start, face) in enumerate(zip(starts, (xa, xb)))
        for i, field in enumerate((wave, born))
    ]
    for copy in copies:
        copy.start()
    for copy in copies:
        copy.wait()


def pack_kernel(place, wave, born, wave_rows, born_rows, ya, yb):
    sub, _ = iotas()
    even_y = place[1] == 0

    def step(x, carry):
        for z in range(TZ):
            w0, w1, b0, b1 = tile(wave, x, 0, z), tile(wave, x, 1, z), tile(born, x, 0, z), tile(born, x, 1, z)
            pack_y(sub, even_y, ya, yb, x, z, w0, w1, b0, b1)
            wave_rows[strip(x, 0, z), :] = w0
            wave_rows[strip(x, 1, z), :] = w1
            born_rows[strip(x, 0, z), :] = b0
            born_rows[strip(x, 1, z), :] = b1
        return carry

    lax.fori_loop(0, CX, step, 0)


def stencil(ref, high, low, z_weights, xy_weights, out):
    zero = jnp.zeros((CX * CY, 128), BF16)
    for half in (high, low):
        half[:, 0:128] = zero
        half[:, 128 + NZ : 256 + NZ] = zero

    def split(x, carry):
        rows = pl.ds(pl.multiple_of(x * CY, CY), CY)
        for z in range(TZ):
            value = ref[pl.ds(pl.multiple_of(x * LAYER + z * STRIP, CY), CY), :]
            top = value.astype(BF16)
            high[rows, 128 + z * 128 : 256 + z * 128] = top
            low[rows, 128 + z * 128 : 256 + z * 128] = (value - top.astype(F32)).astype(BF16)
        return carry

    lax.fori_loop(0, CX, split, 0, unroll=2)
    for c in range(NZ // 256):
        window = slice(c * 256, c * 256 + 512)
        inside = slice(c * 256 + 128, c * 256 + 384)
        wide = jnp.concatenate([high[:, window], low[:, window]], axis=1)
        tall = jnp.concatenate([high[:, inside], low[:, inside]], axis=0)
        twice = jnp.concatenate([xy_weights[...], xy_weights[...]], axis=1)
        out[:, c * 256 : c * 256 + 256] = jnp.dot(wide, z_weights[...], preferred_element_type=F32) + jnp.dot(
            twice, tall, preferred_element_type=F32
        )


def spread(ref, around, x, t, z):
    here = ref[strip(x, t, z), :]
    total = CENTER * here + around[pl.ds(pl.multiple_of(x * CY + t * 8, 8), 8), z * 128 : z * 128 + 128]
    return here, total


def add_sources(cells, amps, contrast, wave_part, born_part):
    sub, lane = iotas()
    for i in range(4):
        cell = cells[i]
        x = lax.shift_right_logical(cell, 14)
        y = lax.bitwise_and(lax.shift_right_logical(cell, 10), 15)
        z = lax.bitwise_and(cell, NZ - 1)
        row = pl.multiple_of(lax.bitwise_and(y, 8), 8)
        col = pl.multiple_of(lax.bitwise_and(z, NZ - 128), 128)
        here = (sub == lax.bitwise_and(y, 7)) & (lane == lax.bitwise_and(z, 127))
        added = jnp.where(here, amps[i], 0.0)
        at = (x, pl.ds(row, 8), pl.ds(col, 128))
        wave_part[at] = wave_part[at] + added
        born_part[at] = born_part[at] + contrast[at] * added


def make_picks(taps, weights, picks):
    lane = lax.broadcasted_iota(jnp.int32, (8, 128), 1)
    for half in range(2):
        spots = lax.bitwise_and(taps[:, half * 128 : half * 128 + 128], 127)
        gains = weights[:, half * 128 : half * 128 + 128]

        def group(g, carry):
            spots, gains = carry
            for j in range(16):
                row = pl.multiple_of((half * 128 + g * 16 + j) * 8, 8)
                picks[pl.ds(row, 8), :] = jnp.where(lane == spots[:, j : j + 1], gains[:, j : j + 1], 0.0)
            return pltpu.roll(spots, 112, 1), pltpu.roll(gains, 112, 1)

        lax.fori_loop(0, 8, group, (spots, gains))


def inner_first(
    cells, amps, wave, born, z_weights, xy_weights, taps, weights, wave_old_in, born_old_in, courant_in, contrast_in,
    wave_part, born_part, courant, contrast, picks, wave_old, born_old, high, low, wave_sum_all, born_sum_all, sems,
):
    copies = [
        pltpu.make_async_copy(a, b, sems.at[i])
        for i, (a, b) in enumerate(
            ((wave_old_in, wave_old), (born_old_in, born_old), (courant_in, courant), (contrast_in, contrast))
        )
    ]
    for copy in copies:
        copy.start()
    stencil(wave, high, low, z_weights, xy_weights, wave_sum_all)
    stencil(born, high, low, z_weights, xy_weights, born_sum_all)
    make_picks(taps, weights, picks)
    for copy in copies:
        copy.wait()

    def step(x, carry):
        for z in range(TZ):
            for t in range(2):
                speed = tile(courant, x, t, z) * (1.0 / SCALE)
                put(courant, x, t, z, speed)
                here, total = spread(wave, wave_sum_all, x, t, z)
                moved = speed * total
                put(wave_part, x, t, z, (2.0 * here - tile(wave_old, x, t, z)) + moved)
                here, total = spread(born, born_sum_all, x, t, z)
                moved = speed * total + tile(contrast, x, t, z) * moved
                put(born_part, x, t, z, (2.0 * here - tile(born_old, x, t, z)) + moved)
        return carry

    lax.fori_loop(0, CX, step, 0)
    add_sources(cells, amps, contrast, wave_part, born_part)


def inner_second(
    cells, amps, rows_at, wave, born, z_weights, xy_weights, wave_old, born_old, courant, contrast, picks, wave_now, born_now,
    wave_part, born_part, first, wave_out, born_out, high, low, wave_sum_all, born_sum_all, rows, sems,
):
    copies = [
        pltpu.make_async_copy(wave_now, wave_out, sems.at[0]),
        pltpu.make_async_copy(born_now, born_out, sems.at[1]),
    ]
    for copy in copies:
        copy.start()
    stencil(wave, high, low, z_weights, xy_weights, wave_sum_all)
    stencil(born, high, low, z_weights, xy_weights, born_sum_all)

    def step(x, carry):
        for z in range(TZ):
            for t in range(2):
                speed = tile(courant, x, t, z)
                here, total = spread(wave, wave_sum_all, x, t, z)
                moved = speed * total
                put(wave_part, x, t, z, (2.0 * here - wave_old[strip(x, t, z), :]) + moved)
                here, total = spread(born, born_sum_all, x, t, z)
                moved = speed * total + tile(contrast, x, t, z) * moved
                put(born_part, x, t, z, (2.0 * here - born_old[strip(x, t, z), :]) + moved)
        return carry

    lax.fori_loop(0, CX, step, 0)
    add_sources(cells, amps, contrast, wave_part, born_part)
    take(rows_at, born, picks, rows, first)
    for copy in copies:
        copy.wait()


def fix(
    place, ends, wave_part, born_part, courant, contrast, xa, xb, ya, yb, wave, born, wave_rows, born_rows, y_faces,
    edges, middle,
):
    sub, _ = iotas()
    even_x = place[0] == 0
    even_y = place[1] == 0
    part = lax.bitwise_and(sub, 3)
    low_weights = [jnp.where(part < k, WEIGHTS[k - 1], 0.0) for k in range(1, 4)]
    high_weights = [jnp.where(part >= 4 - k, WEIGHTS[k - 1], 0.0) for k in range(1, 4)]

    def one(x, side, offset):
        for z in range(TZ):
            from_a, from_b = tile(ya, x, 0, z), tile(yb, x, 0, z)
            low = jnp.where(even_y, from_b, from_a)
            high = jnp.where(even_y, from_a, from_b)
            low_sum, high_sum = WEIGHTS[3] * low, WEIGHTS[3] * high
            for k in range(1, 4):
                low_sum = low_sum + low_weights[k - 1] * pltpu.roll(low, 4 + k, 0)
                high_sum = high_sum + high_weights[k - 1] * pltpu.roll(high, 4 - k, 0)
            wave_sums = [
                jnp.where(sub < 4, low_sum, 0.0),
                jnp.where(sub < 4, 0.0, pltpu.roll(high_sum, 4, 0)),
            ]
            born_sums = [
                jnp.where(sub < 4, pltpu.roll(low_sum, 4, 0), 0.0),
                jnp.where(sub < 4, 0.0, high_sum),
            ]
            finals = []
            for t in range(2):
                wave_sum, born_sum = wave_sums[t], born_sums[t]
                if side:
                    for m in range(4):
                        reach = offset + 4 - m if side < 0 else 4 - offset + m
                        if 1 <= reach <= 4:
                            lone, other = (xb, xa) if side < 0 else (xa, xb)
                            w = WEIGHTS[reach - 1] * ends[0 if side < 0 else 1]
                            wave_sum = wave_sum + w * jnp.where(even_x, tile(lone, m, t, z), tile(other, m, t, z))
                            born_sum = born_sum + w * jnp.where(even_x, tile(lone, m + 4, t, z), tile(other, m + 4, t, z))
                speed = tile(courant, x, t, z)
                moved = speed * wave_sum
                wave_value = tile(wave_part, x, t, z) + moved
                born_value = tile(born_part, x, t, z) + (tile(contrast, x, t, z) * moved + speed * born_sum)
                put(wave, x, t, z, wave_value)
                put(born, x, t, z, born_value)
                if wave_rows is not None:
                    wave_rows[strip(x, t, z), :] = wave_value
                born_rows[strip(x, t, z), :] = born_value
                finals.append((wave_value, born_value))
            if y_faces is not None:
                (w0, b0), (w1, b1) = finals
                pack_y(sub, even_y, *y_faces, x, z, w0, w1, b0, b1)

    if edges:
        for x in range(4):
            one(x, -1, x)
        for x in range(CX - 4, CX):
            one(x, 1, x - (CX - 4))
    if middle:
        lax.fori_loop(4, CX - 4, lambda x, carry: (one(x, 0, 0), carry)[1], 0)


def fix_edges(
    place, ends, wave_part, born_part, courant, contrast, rxa, rxb, rya, ryb,
    wave, born, wave_rows, born_rows, ya, yb, xa, xb,
):
    fix(
        place, ends, wave_part, born_part, courant, contrast, rxa, rxb, rya, ryb,
        wave, born, wave_rows, born_rows, (ya, yb), True, False,
    )
    pack_x(place[0] == 0, xa, xb, wave, born)


def fix_middle(
    place, ends, wave_part, born_part, courant, contrast, rya, ryb, wave_in, born_in, rows_a, rows_b, ya_in, yb_in,
    wave, born, wave_rows, born_rows, ya, yb,
):
    fix(
        place, ends, wave_part, born_part, courant, contrast, None, None, rya, ryb,
        wave, born, wave_rows, born_rows, (ya, yb), False, True,
    )


def take(rows_at, grid, picks, rows, out):
    def step(g, carry):
        for j in range(8):
            r = g * 8 + j
            for t in range(8):
                rows[pl.ds(r * 8 + t, 1), :] = grid[pl.ds(rows_at[t, r], 1), :]
        return carry

    lax.fori_loop(0, 32, step, 0)

    def total(g, carry):
        part = pl.ds(pl.multiple_of(g * 256, 256), 256)
        value = (rows[part, :] * picks[part, :]).reshape(32, 8, 128)
        out[pl.ds(pl.multiple_of(g * 32, 32), 32), :] = jnp.sum(value, axis=1)
        return carry

    lax.fori_loop(0, 8, total, 0)


def last_kernel(
    place, ends, rows_at, wave_part, born_part, courant, contrast, rxa, rxb, rya, ryb,
    picks, first, slots, dest, wave_out, born_out, packed, wave, born, grid, rows, sums, sems,
):
    fix(
        place, ends, wave_part, born_part, courant, contrast, rxa, rxb, rya, ryb,
        wave, born, None, grid, None, True, True,
    )
    copies = [
        pltpu.make_async_copy(wave, wave_out, sems.at[0]),
        pltpu.make_async_copy(born, born_out, sems.at[1]),
    ]
    for copy in copies:
        copy.start()
    take(rows_at, grid, picks, rows, sums)
    one = jnp.sum(first[...], axis=1, keepdims=True)
    two = jnp.sum(sums[...], axis=1, keepdims=True)
    lane = lax.broadcasted_iota(jnp.int32, (256, 128), 1)
    spread_out = jnp.where(lane < 4, one, two) * slots[...]
    owner = lax.broadcasted_iota(jnp.int32, (128, 256), 0)
    chosen = jnp.where(owner == dest[...], 1.0, 0.0).astype(F32)
    packed[...] = jnp.dot(chosen, spread_out, precision=lax.Precision.HIGHEST, preferred_element_type=F32)
    for copy in copies:
        copy.wait()


def pairs(count, first):
    found = []
    for i in range(first, count - 1, 2):
        found += [(i, i + 1), (i + 1, i)]
    return found


VM = pl.BlockSpec(memory_space=pltpu.VMEM)
SM = pl.BlockSpec(memory_space=pltpu.SMEM)
HB = pl.BlockSpec(memory_space=pltpu.HBM)


def kept(shape):
    return VM, pltpu.VMEM(shape, F32)


def plain(shape):
    return VM, jax.ShapeDtypeStruct(shape, F32)


def away(shape):
    return HB, jax.ShapeDtypeStruct(shape, F32)


def still(value):
    return pltpu.with_memory_space_constraint(value, pltpu.HBM)


def call(kernel, args, specs, outs, scratch, mib, us, aliases=None):
    return pl.pallas_call(
        kernel,
        out_shape=tuple(o[1] for o in outs),
        in_specs=specs,
        out_specs=tuple(o[0] for o in outs),
        scratch_shapes=list(scratch),
        input_output_aliases=aliases or {},
        compiler_params=pltpu.CompilerParams(vmem_limit_bytes=mib * 1024 * 1024),
        cost_estimate=pl.CostEstimate(flops=0, bytes_accessed=us * 3_000_000, transcendentals=0),
    )(*args)


def swap_x(xa, xb):
    flat = [(i * 16 + g, j * 16 + g) for i, j in pairs(8, 1) for g in range(16)]
    flat += [(i * 16 + g, i * 16 + (g ^ 1)) for i in (0, 7) for g in range(16)]
    rxb = lax.ppermute(xb, ("gx", "gy"), flat)
    rxa = lax.ppermute(xa, "gx", pairs(8, 0))
    return rxa, rxb


def swap_y(ya, yb):
    ryb = lax.ppermute(yb, "gy", pairs(16, 1))
    rya = lax.ppermute(ya, "gy", pairs(16, 0))
    return rya, ryb


def xy_table():
    size = CX * CY
    row = lax.broadcasted_iota(jnp.int32, (size, size), 0)
    col = lax.broadcasted_iota(jnp.int32, (size, size), 1)
    apart = jnp.abs(row - col)
    along_y = jnp.where(row // CY == col // CY, apart, 0)
    along_x = jnp.where(apart % CY == 0, apart // CY, 0)
    gap = jnp.maximum(along_x, along_y)
    table = jnp.zeros((size, size), F32)
    for k in range(1, 5):
        table = jnp.where(gap == k, WEIGHTS[k - 1], table)
    return table.astype(BF16)


def z_table():
    source = lax.broadcasted_iota(jnp.int32, (1024, 256), 0) % 512 - 128
    target = lax.broadcasted_iota(jnp.int32, (1024, 256), 1)
    gap = jnp.abs(source - target)
    table = jnp.zeros((1024, 256), F32)
    for k in range(1, 5):
        table = jnp.where(gap == k, WEIGHTS[k - 1], table)
    return table.astype(BF16)


def steps(
    wave_old,
    wave_now,
    born_old,
    born_now,
    courant,
    contrast,
    src_cell,
    src_amp,
    rcv_cell,
    rcv_weight,
    rcv_dest,
):
    index_x, index_y = lax.axis_index("gx"), lax.axis_index("gy")
    place = jnp.stack([index_x & 1, index_y & 1]).astype(jnp.int32)
    ends = jnp.stack([index_x > 0, index_x < 7]).astype(F32)
    field = pltpu.VMEM(BLOCK, F32)
    halves = [pltpu.VMEM((CX * CY, NZ + 256), BF16)] * 2 + [pltpu.VMEM((CX * CY, NZ), F32)] * 2
    x_faces, y_faces = [plain(XFACE)] * 2, [plain(YFACE)] * 2
    fixed = [kept(BLOCK)] * 2 + [kept((ROWS, 128))] * 2

    xa, xb, place, ends = call(
        edge_kernel, (place, ends, still(wave_now), still(born_now)), [SM, SM, HB, HB],
        x_faces + [(SM, jax.ShapeDtypeStruct((2,), jnp.int32)), (SM, jax.ShapeDtypeStruct((2,), F32))],
        [pltpu.SemaphoreType.DMA((2, 2))], 4, 1,
    )
    halo_x = swap_x(xa, xb)
    wave_rows, born_rows, ya, yb = call(
        pack_kernel, (place, wave_now, born_now), [SM, VM, VM],
        [kept((ROWS, 128))] * 2 + y_faces, [], 8, 2,
    )
    halo_y = swap_y(ya, yb)
    tables = (z_table(), xy_table())
    wave_part, born_part, speed, factor, picks = call(
        inner_first,
        (
            src_cell, src_amp[:, 0], wave_rows, born_rows, *tables, rcv_cell.T, rcv_weight.T,
            still(wave_old), still(born_old), still(courant), still(contrast),
        ),
        [SM, SM] + [VM] * 6 + [HB] * 4,
        [kept(BLOCK)] * 4 + [kept((2048, 128))], [field, field, *halves, pltpu.SemaphoreType.DMA((4,))], 14, 8,
    )

    cell = rcv_cell.T
    rows_at = (cell >> 14) * LAYER + ((cell >> 7) & 7) * STRIP + ((cell >> 10) & 15)
    dest = rcv_dest[:, 0]
    order = jnp.arange(256, dtype=jnp.int32)
    earlier = (dest[:, None] == dest[None, :]) & (order[None, :] < order[:, None])
    slot = jnp.sum(earlier.astype(jnp.int32), axis=1)
    lane = lax.broadcasted_iota(jnp.int32, (256, 128), 1)
    slots = jnp.where((lane < 8) & (lane % 4 == slot[:, None]), 1.0, 0.0).astype(F32)

    shared = (wave_part, born_part, speed, factor)
    *mid, xa, xb = call(
        fix_edges, (place, ends, *shared, *halo_x, *halo_y),
        [SM] * 2 + [VM] * 8, fixed + y_faces + x_faces, [], 4, 2,
    )
    next_x = swap_x(xa, xb)
    wave_mid, born_mid, wave_mid_rows, born_mid_rows, ya, yb = call(
        fix_middle, (place, ends, *shared, *halo_y, *mid),
        [SM] * 2 + [VM] * 12, fixed + y_faces, [], 4, 2, {i + 8: i for i in range(6)},
    )
    next_y = swap_y(ya, yb)
    wave_part, born_part, first, wave_next, born_next = call(
        inner_second,
        (
            src_cell, src_amp[:, 1], rows_at, wave_mid_rows, born_mid_rows, *tables, wave_rows, born_rows,
            speed, factor, picks, wave_mid, born_mid,
        ),
        [SM] * 3 + [VM] * 11,
        [kept(BLOCK)] * 2 + [plain((256, 128)), away(BLOCK), away(BLOCK)],
        [*halves, pltpu.VMEM((2048, 128), F32), pltpu.SemaphoreType.DMA((2,))], 12, 10,
    )
    wave_last, born_last, packed = call(
        last_kernel,
        (place, ends, rows_at, wave_part, born_part, speed, factor, *next_x, *next_y, picks, first, slots, dest[None, :]),
        [SM] * 3 + [VM] * 12,
        [away(BLOCK), away(BLOCK), plain((128, 128))],
        [
            field, field, pltpu.VMEM((ROWS, 128), F32), pltpu.VMEM((2048, 128), F32),
            pltpu.VMEM((256, 128), F32), pltpu.SemaphoreType.DMA((2,)),
        ], 16, 5,
    )
    arrived = lax.all_to_all(
        packed.reshape(128, 1, 128), ("gx", "gy"), split_axis=0, concat_axis=0, tiled=True
    )
    gathers = arrived[:, 0, :8].reshape(1, 128, 2, CAP)
    return (wave_next, wave_last, born_next, born_last, gathers)


def solution(mesh):
    placed = (P("gx", "gy", None),) * 6 + (
        P(("gx", "gy")),
        P(("gx", "gy"), None),
        P(("gx", "gy"), None),
        P(("gx", "gy"), None),
        P(("gx", "gy"), None),
    )
    return jax.shard_map(
        steps,
        mesh=mesh,
        in_specs=placed,
        out_specs=(P("gx", "gy", None),) * 4 + (P(("gx", "gy"), None, None, None),),
        check_vma=False,
    )
```

```python
import jax
import jax.numpy as jnp
from jax import lax
from jax.experimental import pallas as pl
from jax.experimental.pallas import tpu as pltpu
from jax.sharding import PartitionSpec as P


CAP = 4
SCALE = 5040.0
CENTER = -3.0 * 14350.0
WEIGHTS = (8064.0, -1008.0, 128.0, -9.0)
CX, CY, NZ = 32, 16, 1024
TZ = NZ // 128
BLOCK = (CX, CY, NZ)
XFACE = (8, CY, NZ)
YFACE = (CX, 8, NZ)
STRIP = CY
LAYER = TZ * STRIP
ROWS = CX * LAYER
F32 = jnp.float32
BF16 = jnp.bfloat16


def iotas():
    sub = lax.broadcasted_iota(jnp.int32, (8, 128), 0)
    lane = lax.broadcasted_iota(jnp.int32, (8, 128), 1)
    return sub, lane


def tile(ref, x, t, z):
    return ref[x, t * 8 : t * 8 + 8, z * 128 : z * 128 + 128]


def put(ref, x, t, z, value):
    ref[x, t * 8 : t * 8 + 8, z * 128 : z * 128 + 128] = value


def strip(x, t, z):
    return pl.ds(pl.multiple_of(x * LAYER + (z * STRIP + t * 8), 8), 8)


def pack_y(sub, even, ya, yb, x, z, w0, w1, b0, b1):
    low = jnp.where(sub < 4, w0, pltpu.roll(b0, 4, 0))
    high = jnp.where(sub < 4, pltpu.roll(w1, 4, 0), b1)
    put(ya, x, 0, z, jnp.where(even, high, low))
    put(yb, x, 0, z, jnp.where(even, low, high))


def pack_x(even, xa, xb, wave, born):
    start_a = jnp.where(even, CX - 4, 0)
    start_b = jnp.where(even, 0, CX - 4)
    for i in range(4):
        xa[i] = wave[start_a + i]
        xa[i + 4] = born[start_a + i]
        xb[i] = wave[start_b + i]
        xb[i + 4] = born[start_b + i]


def edge_kernel(place, ends, wave, born, xa, xb, place_out, ends_out, sems):
    for i in range(2):
        place_out[i] = place[i]
        ends_out[i] = ends[i]
    even = place[0] == 0
    starts = (jnp.where(even, CX - 4, 0), jnp.where(even, 0, CX - 4))
    copies = [
        pltpu.make_async_copy(field.at[pl.ds(start, 4)], face.at[pl.ds(4 * i, 4)], sems.at[j, i])
        for j, (start, face) in enumerate(zip(starts, (xa, xb)))
        for i, field in enumerate((wave, born))
    ]
    for copy in copies:
        copy.start()
    for copy in copies:
        copy.wait()


def pack_kernel(place, wave, born, wave_rows, born_rows, ya, yb):
    sub, _ = iotas()
    even_y = place[1] == 0

    def step(x, carry):
        for z in range(TZ):
            w0, w1, b0, b1 = tile(wave, x, 0, z), tile(wave, x, 1, z), tile(born, x, 0, z), tile(born, x, 1, z)
            pack_y(sub, even_y, ya, yb, x, z, w0, w1, b0, b1)
            wave_rows[strip(x, 0, z), :] = w0
            wave_rows[strip(x, 1, z), :] = w1
            born_rows[strip(x, 0, z), :] = b0
            born_rows[strip(x, 1, z), :] = b1
        return carry

    lax.fori_loop(0, CX, step, 0)


def stencil(ref, high, low, z_weights, xy_weights, out):
    zero = jnp.zeros((CX * CY, 128), BF16)
    for half in (high, low):
        half[:, 0:128] = zero
        half[:, 128 + NZ : 256 + NZ] = zero

    def split(x, carry):
        rows = pl.ds(pl.multiple_of(x * CY, CY), CY)
        for z in range(TZ):
            value = ref[pl.ds(pl.multiple_of(x * LAYER + z * STRIP, CY), CY), :]
            top = value.astype(BF16)
            high[rows, 128 + z * 128 : 256 + z * 128] = top
            low[rows, 128 + z * 128 : 256 + z * 128] = (value - top.astype(F32)).astype(BF16)
        return carry

    lax.fori_loop(0, CX, split, 0, unroll=2)
    for c in range(NZ // 256):
        window = slice(c * 256, c * 256 + 512)
        inside = slice(c * 256 + 128, c * 256 + 384)
        wide = jnp.concatenate([high[:, window], low[:, window]], axis=1)
        tall = jnp.concatenate([high[:, inside], low[:, inside]], axis=0)
        twice = jnp.concatenate([xy_weights[...], xy_weights[...]], axis=1)
        out[:, c * 256 : c * 256 + 256] = jnp.dot(wide, z_weights[...], preferred_element_type=F32) + jnp.dot(
            twice, tall, preferred_element_type=F32
        )


def spread(ref, around, x, t, z):
    here = ref[strip(x, t, z), :]
    total = CENTER * here + around[pl.ds(pl.multiple_of(x * CY + t * 8, 8), 8), z * 128 : z * 128 + 128]
    return here, total


def add_sources(cells, amps, contrast, wave_part, born_part):
    sub, lane = iotas()
    for i in range(4):
        cell = cells[i]
        x = lax.shift_right_logical(cell, 14)
        y = lax.bitwise_and(lax.shift_right_logical(cell, 10), 15)
        z = lax.bitwise_and(cell, NZ - 1)
        row = pl.multiple_of(lax.bitwise_and(y, 8), 8)
        col = pl.multiple_of(lax.bitwise_and(z, NZ - 128), 128)
        here = (sub == lax.bitwise_and(y, 7)) & (lane == lax.bitwise_and(z, 127))
        added = jnp.where(here, amps[i], 0.0)
        at = (x, pl.ds(row, 8), pl.ds(col, 128))
        wave_part[at] = wave_part[at] + added
        born_part[at] = born_part[at] + contrast[at] * added


def make_picks(taps, weights, picks):
    lane = lax.broadcasted_iota(jnp.int32, (8, 128), 1)
    for half in range(2):
        spots = lax.bitwise_and(taps[:, half * 128 : half * 128 + 128], 127)
        gains = weights[:, half * 128 : half * 128 + 128]

        def group(g, carry):
            spots, gains = carry
            for j in range(16):
                row = pl.multiple_of((half * 128 + g * 16 + j) * 8, 8)
                picks[pl.ds(row, 8), :] = jnp.where(lane == spots[:, j : j + 1], gains[:, j : j + 1], 0.0)
            return pltpu.roll(spots, 112, 1), pltpu.roll(gains, 112, 1)

        lax.fori_loop(0, 8, group, (spots, gains))


def inner_first(
    cells, amps, wave, born, z_weights, xy_weights, taps, weights, wave_old_in, born_old_in, courant_in, contrast_in,
    wave_part, born_part, courant, contrast, picks, wave_old, born_old, high, low, wave_sum_all, born_sum_all, sems,
):
    copies = [
        pltpu.make_async_copy(a, b, sems.at[i])
        for i, (a, b) in enumerate(
            ((wave_old_in, wave_old), (born_old_in, born_old), (courant_in, courant), (contrast_in, contrast))
        )
    ]
    for copy in copies:
        copy.start()
    stencil(wave, high, low, z_weights, xy_weights, wave_sum_all)
    stencil(born, high, low, z_weights, xy_weights, born_sum_all)
    make_picks(taps, weights, picks)
    for copy in copies:
        copy.wait()

    def step(x, carry):
        for z in range(TZ):
            for t in range(2):
                speed = tile(courant, x, t, z) * (1.0 / SCALE)
                put(courant, x, t, z, speed)
                here, total = spread(wave, wave_sum_all, x, t, z)
                moved = speed * total
                put(wave_part, x, t, z, (2.0 * here - tile(wave_old, x, t, z)) + moved)
                here, total = spread(born, born_sum_all, x, t, z)
                moved = speed * total + tile(contrast, x, t, z) * moved
                put(born_part, x, t, z, (2.0 * here - tile(born_old, x, t, z)) + moved)
        return carry

    lax.fori_loop(0, CX, step, 0)
    add_sources(cells, amps, contrast, wave_part, born_part)


def inner_second(
    cells, amps, rows_at, wave, born, z_weights, xy_weights, wave_old, born_old, courant, contrast, picks, slots, wave_now, born_now,
    wave_part, born_part, first, wave_out, born_out, high, low, wave_sum_all, born_sum_all, rows, sums, sems,
):
    copies = [
        pltpu.make_async_copy(wave_now, wave_out, sems.at[0]),
        pltpu.make_async_copy(born_now, born_out, sems.at[1]),
    ]
    for copy in copies:
        copy.start()
    stencil(wave, high, low, z_weights, xy_weights, wave_sum_all)
    stencil(born, high, low, z_weights, xy_weights, born_sum_all)

    def step(x, carry):
        for z in range(TZ):
            for t in range(2):
                speed = tile(courant, x, t, z)
                here, total = spread(wave, wave_sum_all, x, t, z)
                moved = speed * total
                put(wave_part, x, t, z, (2.0 * here - wave_old[strip(x, t, z), :]) + moved)
                here, total = spread(born, born_sum_all, x, t, z)
                moved = speed * total + tile(contrast, x, t, z) * moved
                put(born_part, x, t, z, (2.0 * here - born_old[strip(x, t, z), :]) + moved)
        return carry

    lax.fori_loop(0, CX, step, 0)
    add_sources(cells, amps, contrast, wave_part, born_part)
    take(rows_at, born, picks, rows, sums)
    lane = lax.broadcasted_iota(jnp.int32, (256, 128), 1)
    first[...] = jnp.where(lane < 4, jnp.sum(sums[...], axis=1, keepdims=True), 0.0) * slots[...]
    for copy in copies:
        copy.wait()


def fix(place, ends, parts, scales, x_halo, y_halo, outs, y_faces, edges, middle, tiles=(0, 1)):
    wave_part, born_part = parts
    courant, contrast = scales
    wave, born, wave_rows, born_rows = outs
    sub, _ = iotas()
    even_x = place[0] == 0
    even_y = place[1] == 0
    part = lax.bitwise_and(sub, 3)

    low_weights = [jnp.where(part < k, WEIGHTS[k - 1], 0.0) for k in range(1, 4)]
    high_weights = [jnp.where(part >= 4 - k, WEIGHTS[k - 1], 0.0) for k in range(1, 4)]

    def one(x, side, offset):
        for z in range(TZ):
            low, high = y_halo(x, z)
            wave_sums, born_sums = [None, None], [None, None]
            if low is not None:
                total = WEIGHTS[3] * low
                for k in range(1, 4):
                    total = total + low_weights[k - 1] * pltpu.roll(low, 4 + k, 0)
                wave_sums[0] = jnp.where(sub < 4, total, 0.0)
                born_sums[0] = jnp.where(sub < 4, pltpu.roll(total, 4, 0), 0.0)
            if high is not None:
                total = WEIGHTS[3] * high
                for k in range(1, 4):
                    total = total + high_weights[k - 1] * pltpu.roll(high, 4 - k, 0)
                wave_sums[1] = jnp.where(sub < 4, 0.0, pltpu.roll(total, 4, 0))
                born_sums[1] = jnp.where(sub < 4, 0.0, total)
            finals = []
            for t in tiles:
                wave_sum, born_sum = wave_sums[t], born_sums[t]
                if side:
                    for m in range(4):
                        reach = offset + 4 - m if side < 0 else 4 - offset + m
                        if 1 <= reach <= 4:
                            lone, other = (x_halo[1], x_halo[0]) if side < 0 else x_halo
                            w = WEIGHTS[reach - 1] * ends[0 if side < 0 else 1]
                            wave_term = w * jnp.where(even_x, tile(lone, m, t, z), tile(other, m, t, z))
                            born_term = w * jnp.where(even_x, tile(lone, m + 4, t, z), tile(other, m + 4, t, z))
                            wave_sum = wave_term if wave_sum is None else wave_sum + wave_term
                            born_sum = born_term if born_sum is None else born_sum + born_term
                wave_value, born_value = tile(wave_part, x, t, z), tile(born_part, x, t, z)
                if wave_sum is not None:
                    speed = tile(courant, x, t, z)
                    moved = speed * wave_sum
                    wave_value = wave_value + moved
                    born_value = born_value + (tile(contrast, x, t, z) * moved + speed * born_sum)
                put(wave, x, t, z, wave_value)
                put(born, x, t, z, born_value)
                if wave_rows is not None:
                    wave_rows[strip(x, t, z), :] = wave_value
                born_rows[strip(x, t, z), :] = born_value
                finals.append((wave_value, born_value))
            if y_faces is not None:
                (w0, b0), (w1, b1) = finals
                pack_y(sub, even_y, *y_faces, x, z, w0, w1, b0, b1)

    if edges:
        for x in range(4):
            one(x, -1, x)
        for x in range(CX - 4, CX):
            one(x, 1, x - (CX - 4))
    if middle:
        first, end = middle
        lax.fori_loop(first, end, lambda x, carry: (one(x, 0, 0), carry)[1], 0)


def both_sides(place, ya, yb):
    even_y = place[1] == 0

    def pick(x, z):
        from_a, from_b = tile(ya, x, 0, z), tile(yb, x, 0, z)
        return jnp.where(even_y, from_b, from_a), jnp.where(even_y, from_a, from_b)

    return pick


def low_side(face):
    return lambda x, z: (tile(face, x, 0, z), None)


def high_side(face):
    return lambda x, z: (None, tile(face, x, 0, z))


def fix_edges(
    place, ends, wave_part, born_part, courant, contrast, rxa, rxb, rya, ryb,
    wave, born, wave_rows, born_rows, ya, yb, xa, xb,
):
    fix(
        place, ends, (wave_part, born_part), (courant, contrast), (rxa, rxb), both_sides(place, rya, ryb),
        (wave, born, wave_rows, born_rows), (ya, yb), True, None,
    )
    pack_x(place[0] == 0, xa, xb, wave, born)


def fix_middle(
    place, ends, wave_part, born_part, courant, contrast, rya, ryb, wave_in, born_in, rows_a, rows_b, ya_in, yb_in,
    wave, born, wave_rows, born_rows, ya, yb,
):
    fix(
        place, ends, (wave_part, born_part), (courant, contrast), None, both_sides(place, rya, ryb),
        (wave, born, wave_rows, born_rows), (ya, yb), False, (4, CX - 4),
    )


def fix_early(
    place, ends, wave_part, born_part, courant, contrast, rxa, rxb, rya, wave, born, born_rows,
):
    for even in (True, False):

        @pl.when((place[1] == 0) == even)
        def _():
            fix(
                place, ends, (wave_part, born_part), (courant, contrast), (rxa, rxb),
                high_side(rya) if even else low_side(rya),
                (wave, born, None, born_rows), None, True, (4, CX - 4),
            )


def take(rows_at, grid, picks, rows, out):
    def step(g, carry):
        for half in range(2):
            for j in range(8):
                for t in range(8):
                    source = rows_at[g * 8 + (half * 1024 + t * 128 + j)]
                    rows[pl.ds(g * 64 + (half * 1024 + j * 8 + t), 1), :] = grid[pl.ds(source, 1), :]
        return carry

    lax.fori_loop(0, 16, step, 0)

    def total(g, carry):
        part = pl.ds(pl.multiple_of(g * 256, 256), 256)
        value = (rows[part, :] * picks[part, :]).reshape(32, 8, 128)
        out[pl.ds(pl.multiple_of(g * 32, 32), 32), :] = jnp.sum(value, axis=1)
        return carry

    lax.fori_loop(0, 8, total, 0)


def last_kernel(
    place, rows_at, wave_in, born_in, grid_in, courant, contrast, ryb, picks, first, slots, dest,
    wave, born, grid, wave_out, born_out, packed, rows, sums, sems,
):
    for even in (True, False):

        @pl.when((place[1] == 0) == even)
        def _():
            fix(
                place, None, (wave_in, born_in), (courant, contrast), None,
                low_side(ryb) if even else high_side(ryb),
                (wave, born, None, grid), None, False, (0, CX), (0,) if even else (1,),
            )

    copies = [
        pltpu.make_async_copy(wave, wave_out, sems.at[0]),
        pltpu.make_async_copy(born, born_out, sems.at[1]),
    ]
    for copy in copies:
        copy.start()
    take(rows_at, grid, picks, rows, sums)
    two = jnp.sum(sums[...], axis=1, keepdims=True)
    lane = lax.broadcasted_iota(jnp.int32, (256, 128), 1)
    spread_out = first[...] + jnp.where(lane < 4, 0.0, two) * slots[...]
    owner = lax.broadcasted_iota(jnp.int32, (128, 256), 0)
    chosen = jnp.where(owner == dest[...], 1.0, 0.0).astype(F32)
    packed[...] = jnp.dot(chosen, spread_out, precision=lax.Precision.HIGHEST, preferred_element_type=F32)
    for copy in copies:
        copy.wait()


def pairs(count, first):
    found = []
    for i in range(first, count - 1, 2):
        found += [(i, i + 1), (i + 1, i)]
    return found


VM = pl.BlockSpec(memory_space=pltpu.VMEM)
SM = pl.BlockSpec(memory_space=pltpu.SMEM)
HB = pl.BlockSpec(memory_space=pltpu.HBM)


def kept(shape):
    return VM, pltpu.VMEM(shape, F32)


def plain(shape):
    return VM, jax.ShapeDtypeStruct(shape, F32)


def away(shape):
    return HB, jax.ShapeDtypeStruct(shape, F32)


def still(value):
    return pltpu.with_memory_space_constraint(value, pltpu.HBM)


def call(kernel, args, specs, outs, scratch, mib, us, aliases=None):
    return pl.pallas_call(
        kernel,
        out_shape=tuple(o[1] for o in outs),
        in_specs=specs,
        out_specs=tuple(o[0] for o in outs),
        scratch_shapes=list(scratch),
        input_output_aliases=aliases or {},
        compiler_params=pltpu.CompilerParams(vmem_limit_bytes=mib * 1024 * 1024),
        cost_estimate=pl.CostEstimate(flops=0, bytes_accessed=us * 3_000_000, transcendentals=0),
    )(*args)


def swap_x(xa, xb):
    flat = [(i * 16 + g, j * 16 + g) for i, j in pairs(8, 1) for g in range(16)]
    flat += [(i * 16 + g, i * 16 + (g ^ 1)) for i in (0, 7) for g in range(16)]
    rxb = lax.ppermute(xb, ("gx", "gy"), flat)
    rxa = lax.ppermute(xa, "gx", pairs(8, 0))
    return rxa, rxb


def swap_y(ya, yb):
    ryb = lax.ppermute(yb, "gy", pairs(16, 1))
    rya = lax.ppermute(ya, "gy", pairs(16, 0))
    return rya, ryb


def xy_table():
    size = CX * CY
    row = lax.broadcasted_iota(jnp.int32, (size, size), 0)
    col = lax.broadcasted_iota(jnp.int32, (size, size), 1)
    apart = jnp.abs(row - col)
    along_y = jnp.where(row // CY == col // CY, apart, 0)
    along_x = jnp.where(apart % CY == 0, apart // CY, 0)
    gap = jnp.maximum(along_x, along_y)
    table = jnp.zeros((size, size), F32)
    for k in range(1, 5):
        table = jnp.where(gap == k, WEIGHTS[k - 1], table)
    return table.astype(BF16)


def z_table():
    source = lax.broadcasted_iota(jnp.int32, (1024, 256), 0) % 512 - 128
    target = lax.broadcasted_iota(jnp.int32, (1024, 256), 1)
    gap = jnp.abs(source - target)
    table = jnp.zeros((1024, 256), F32)
    for k in range(1, 5):
        table = jnp.where(gap == k, WEIGHTS[k - 1], table)
    return table.astype(BF16)


def steps(
    wave_old,
    wave_now,
    born_old,
    born_now,
    courant,
    contrast,
    src_cell,
    src_amp,
    rcv_cell,
    rcv_weight,
    rcv_dest,
):
    index_x, index_y = lax.axis_index("gx"), lax.axis_index("gy")
    place = jnp.stack([index_x & 1, index_y & 1]).astype(jnp.int32)
    ends = jnp.stack([index_x > 0, index_x < 7]).astype(F32)
    field = pltpu.VMEM(BLOCK, F32)
    halves = [pltpu.VMEM((CX * CY, NZ + 256), BF16)] * 2 + [pltpu.VMEM((CX * CY, NZ), F32)] * 2
    x_faces, y_faces = [plain(XFACE)] * 2, [plain(YFACE)] * 2
    fixed = [kept(BLOCK)] * 2 + [kept((ROWS, 128))] * 2

    xa, xb, place, ends = call(
        edge_kernel, (place, ends, still(wave_now), still(born_now)), [SM, SM, HB, HB],
        x_faces + [(SM, jax.ShapeDtypeStruct((2,), jnp.int32)), (SM, jax.ShapeDtypeStruct((2,), F32))],
        [pltpu.SemaphoreType.DMA((2, 2))], 4, 1,
    )
    halo_x = swap_x(xa, xb)
    wave_rows, born_rows, ya, yb = call(
        pack_kernel, (place, wave_now, born_now), [SM, VM, VM],
        [kept((ROWS, 128))] * 2 + y_faces, [], 8, 2,
    )
    halo_y = swap_y(ya, yb)
    tables = (z_table(), xy_table())
    wave_part, born_part, speed, factor, picks = call(
        inner_first,
        (
            src_cell, src_amp[:, 0], wave_rows, born_rows, *tables, rcv_cell.T, rcv_weight.T,
            still(wave_old), still(born_old), still(courant), still(contrast),
        ),
        [SM, SM] + [VM] * 6 + [HB] * 4,
        [kept(BLOCK)] * 4 + [kept((2048, 128))], [field, field, *halves, pltpu.SemaphoreType.DMA((4,))], 14, 8,
    )

    cell = rcv_cell.T
    rows_at = (cell >> 14) * LAYER + ((cell >> 7) & 7) * STRIP + ((cell >> 10) & 15)
    rows_at = rows_at.reshape(8, 2, 128).transpose(1, 0, 2).reshape(2048)
    dest = rcv_dest[:, 0]
    order = jnp.arange(256, dtype=jnp.int32)
    earlier = (dest[:, None] == dest[None, :]) & (order[None, :] < order[:, None])
    slot = jnp.sum(earlier.astype(jnp.int32), axis=1)
    lane = lax.broadcasted_iota(jnp.int32, (256, 128), 1)
    slots = jnp.where((lane < 8) & (lane % 4 == slot[:, None]), 1.0, 0.0).astype(F32)

    shared = (wave_part, born_part, speed, factor)
    *mid, xa, xb = call(
        fix_edges, (place, ends, *shared, *halo_x, *halo_y),
        [SM] * 2 + [VM] * 8, fixed + y_faces + x_faces, [], 4, 2,
    )
    next_x = swap_x(xa, xb)
    wave_mid, born_mid, wave_mid_rows, born_mid_rows, ya, yb = call(
        fix_middle, (place, ends, *shared, *halo_y, *mid),
        [SM] * 2 + [VM] * 12, fixed + y_faces, [], 4, 2, {i + 8: i for i in range(6)},
    )
    next_y = swap_y(ya, yb)
    wave_part, born_part, first, wave_next, born_next = call(
        inner_second,
        (
            src_cell, src_amp[:, 1], rows_at, wave_mid_rows, born_mid_rows, *tables, wave_rows, born_rows,
            speed, factor, picks, slots, wave_mid, born_mid,
        ),
        [SM] * 3 + [VM] * 12,
        [kept(BLOCK)] * 2 + [plain((256, 128)), away(BLOCK), away(BLOCK)],
        [*halves, pltpu.VMEM((2048, 128), F32), pltpu.VMEM((256, 128), F32), pltpu.SemaphoreType.DMA((2,))], 12, 10,
    )
    near = call(
        fix_early, (place, ends, wave_part, born_part, speed, factor, *next_x, next_y[0]),
        [SM] * 2 + [VM] * 7, [kept(BLOCK)] * 2 + [kept((ROWS, 128))], [], 4, 3, {2: 0, 3: 1},
    )
    *_, wave_last, born_last, packed = call(
        last_kernel,
        (place, rows_at, *near, speed, factor, next_y[1], picks, first, slots, dest[None, :]),
        [SM] * 2 + [VM] * 10,
        [kept(BLOCK)] * 2 + [kept((ROWS, 128)), away(BLOCK), away(BLOCK), plain((128, 128))],
        [pltpu.VMEM((2048, 128), F32), pltpu.VMEM((256, 128), F32), pltpu.SemaphoreType.DMA((2,))],
        8, 4, {2: 0, 3: 1, 4: 2},
    )
    arrived = lax.all_to_all(
        packed.reshape(128, 1, 128), ("gx", "gy"), split_axis=0, concat_axis=0, tiled=True
    )
    gathers = arrived[:, 0, :8].reshape(1, 128, 2, CAP)
    return (wave_next, wave_last, born_next, born_last, gathers)


def solution(mesh):
    placed = (P("gx", "gy", None),) * 6 + (
        P(("gx", "gy")),
        P(("gx", "gy"), None),
        P(("gx", "gy"), None),
        P(("gx", "gy"), None),
        P(("gx", "gy"), None),
    )
    return jax.shard_map(
        steps,
        mesh=mesh,
        in_specs=placed,
        out_specs=(P("gx", "gy", None),) * 4 + (P(("gx", "gy"), None, None, None),),
        check_vma=False,
    )
```

```python
import jax
import jax.numpy as jnp
from jax import lax
from jax.experimental import pallas as pl
from jax.experimental.pallas import tpu as pltpu
from jax.sharding import PartitionSpec as P


CAP = 4
SCALE = 5040.0
CENTER = -3.0 * 14350.0
WEIGHTS = (8064.0, -1008.0, 128.0, -9.0)
CX, CY, NZ = 32, 16, 1024
TZ = NZ // 128
BLOCK = (CX, CY, NZ)
XFACE = (8, CY, NZ)
YFACE = (CX, 8, NZ)
STRIP = CY
LAYER = TZ * STRIP
ROWS = CX * LAYER
F32 = jnp.float32
BF16 = jnp.bfloat16


def iotas():
    sub = lax.broadcasted_iota(jnp.int32, (8, 128), 0)
    lane = lax.broadcasted_iota(jnp.int32, (8, 128), 1)
    return sub, lane


def tile(ref, x, t, z):
    return ref[x, t * 8 : t * 8 + 8, z * 128 : z * 128 + 128]


def put(ref, x, t, z, value):
    ref[x, t * 8 : t * 8 + 8, z * 128 : z * 128 + 128] = value


def strip(x, t, z):
    return pl.ds(pl.multiple_of(x * LAYER + (z * STRIP + t * 8), 8), 8)


def pack_y(sub, even, ya, yb, x, z, w0, w1, b0, b1):
    low = jnp.where(sub < 4, w0, pltpu.roll(b0, 4, 0))
    high = jnp.where(sub < 4, pltpu.roll(w1, 4, 0), b1)
    put(ya, x, 0, z, jnp.where(even, high, low))
    put(yb, x, 0, z, jnp.where(even, low, high))


def pack_x(even, xa, xb, wave, born):
    start_a = jnp.where(even, CX - 4, 0)
    start_b = jnp.where(even, 0, CX - 4)
    for i in range(4):
        xa[i] = wave[start_a + i]
        xa[i + 4] = born[start_a + i]
        xb[i] = wave[start_b + i]
        xb[i + 4] = born[start_b + i]


def edge_kernel(place, ends, wave, born, xa, xb, place_out, ends_out, sems):
    for i in range(2):
        place_out[i] = place[i]
        ends_out[i] = ends[i]
    even = place[0] == 0
    starts = (jnp.where(even, CX - 4, 0), jnp.where(even, 0, CX - 4))
    copies = [
        pltpu.make_async_copy(field.at[pl.ds(start, 4)], face.at[pl.ds(4 * i, 4)], sems.at[j, i])
        for j, (start, face) in enumerate(zip(starts, (xa, xb)))
        for i, field in enumerate((wave, born))
    ]
    for copy in copies:
        copy.start()
    for copy in copies:
        copy.wait()


def pack_kernel(place, wave, born, wave_rows, born_rows, ya, yb):
    sub, _ = iotas()
    even_y = place[1] == 0

    def step(x, carry):
        for z in range(TZ):
            w0, w1, b0, b1 = tile(wave, x, 0, z), tile(wave, x, 1, z), tile(born, x, 0, z), tile(born, x, 1, z)
            pack_y(sub, even_y, ya, yb, x, z, w0, w1, b0, b1)
            wave_rows[strip(x, 0, z), :] = w0
            wave_rows[strip(x, 1, z), :] = w1
            born_rows[strip(x, 0, z), :] = b0
            born_rows[strip(x, 1, z), :] = b1
        return carry

    lax.fori_loop(0, CX, step, 0)


def stencil(ref, high, low, z_weights, xy_weights, out):
    zero = jnp.zeros((CX * CY, 128), BF16)
    for half in (high, low):
        half[:, 0:128] = zero
        half[:, 128 + NZ : 256 + NZ] = zero

    def split(x, carry):
        rows = pl.ds(pl.multiple_of(x * CY, CY), CY)
        for z in range(TZ):
            value = ref[pl.ds(pl.multiple_of(x * LAYER + z * STRIP, CY), CY), :]
            top = value.astype(BF16)
            high[rows, 128 + z * 128 : 256 + z * 128] = top
            low[rows, 128 + z * 128 : 256 + z * 128] = (value - top.astype(F32)).astype(BF16)
        return carry

    lax.fori_loop(0, CX, split, 0, unroll=2)
    for c in range(NZ // 256):
        window = slice(c * 256, c * 256 + 512)
        inside = slice(c * 256 + 128, c * 256 + 384)
        wide = jnp.concatenate([high[:, window], low[:, window]], axis=1)
        tall = jnp.concatenate([high[:, inside], low[:, inside]], axis=0)
        twice = jnp.concatenate([xy_weights[...], xy_weights[...]], axis=1)
        out[:, c * 256 : c * 256 + 256] = jnp.dot(wide, z_weights[...], preferred_element_type=F32) + jnp.dot(
            twice, tall, preferred_element_type=F32
        )


def spread(ref, around, x, t, z):
    here = ref[strip(x, t, z), :]
    total = CENTER * here + around[pl.ds(pl.multiple_of(x * CY + t * 8, 8), 8), z * 128 : z * 128 + 128]
    return here, total


def add_sources(cells, amps, contrast, wave_part, born_part):
    sub, lane = iotas()
    for i in range(4):
        cell = cells[i]
        x = lax.shift_right_logical(cell, 14)
        y = lax.bitwise_and(lax.shift_right_logical(cell, 10), 15)
        z = lax.bitwise_and(cell, NZ - 1)
        row = pl.multiple_of(lax.bitwise_and(y, 8), 8)
        col = pl.multiple_of(lax.bitwise_and(z, NZ - 128), 128)
        here = (sub == lax.bitwise_and(y, 7)) & (lane == lax.bitwise_and(z, 127))
        added = jnp.where(here, amps[i], 0.0)
        at = (x, pl.ds(row, 8), pl.ds(col, 128))
        wave_part[at] = wave_part[at] + added
        born_part[at] = born_part[at] + contrast[at] * added


def make_picks(taps, weights, picks):
    lane = lax.broadcasted_iota(jnp.int32, (8, 128), 1)
    for half in range(2):
        spots = lax.bitwise_and(taps[:, half * 128 : half * 128 + 128], 127)
        gains = weights[:, half * 128 : half * 128 + 128]

        def group(g, carry):
            spots, gains = carry
            for j in range(16):
                row = pl.multiple_of((half * 128 + g * 16 + j) * 8, 8)
                picks[pl.ds(row, 8), :] = jnp.where(lane == spots[:, j : j + 1], gains[:, j : j + 1], 0.0)
            return pltpu.roll(spots, 112, 1), pltpu.roll(gains, 112, 1)

        lax.fori_loop(0, 8, group, (spots, gains))


def inner_first(
    cells, amps, wave, born, z_weights, xy_weights, taps, weights, wave_old_in, born_old_in, courant_in, contrast_in,
    wave_part, born_part, courant, contrast, picks, wave_old, born_old, high, low, wave_sum_all, born_sum_all, sems,
):
    copies = [
        pltpu.make_async_copy(a, b, sems.at[i])
        for i, (a, b) in enumerate(
            ((wave_old_in, wave_old), (born_old_in, born_old), (courant_in, courant), (contrast_in, contrast))
        )
    ]
    for copy in copies:
        copy.start()
    stencil(wave, high, low, z_weights, xy_weights, wave_sum_all)
    stencil(born, high, low, z_weights, xy_weights, born_sum_all)
    make_picks(taps, weights, picks)
    for copy in copies:
        copy.wait()

    def step(x, carry):
        for z in range(TZ):
            for t in range(2):
                speed = tile(courant, x, t, z) * (1.0 / SCALE)
                put(courant, x, t, z, speed)
                here, total = spread(wave, wave_sum_all, x, t, z)
                moved = speed * total
                put(wave_part, x, t, z, (2.0 * here - tile(wave_old, x, t, z)) + moved)
                here, total = spread(born, born_sum_all, x, t, z)
                moved = speed * total + tile(contrast, x, t, z) * moved
                put(born_part, x, t, z, (2.0 * here - tile(born_old, x, t, z)) + moved)
        return carry

    lax.fori_loop(0, CX, step, 0)
    add_sources(cells, amps, contrast, wave_part, born_part)


def inner_second(
    cells, amps, rows_at, wave, born, z_weights, xy_weights, wave_old, born_old, courant, contrast, picks, slots, wave_now, born_now,
    wave_part, born_part, first, wave_out, born_out, high, low, wave_sum_all, born_sum_all, rows, sums, sems,
):
    copies = [
        pltpu.make_async_copy(wave_now, wave_out, sems.at[0]),
        pltpu.make_async_copy(born_now, born_out, sems.at[1]),
    ]
    for copy in copies:
        copy.start()
    stencil(wave, high, low, z_weights, xy_weights, wave_sum_all)
    stencil(born, high, low, z_weights, xy_weights, born_sum_all)

    def step(x, carry):
        for z in range(TZ):
            for t in range(2):
                speed = tile(courant, x, t, z)
                here, total = spread(wave, wave_sum_all, x, t, z)
                moved = speed * total
                put(wave_part, x, t, z, (2.0 * here - wave_old[strip(x, t, z), :]) + moved)
                here, total = spread(born, born_sum_all, x, t, z)
                moved = speed * total + tile(contrast, x, t, z) * moved
                put(born_part, x, t, z, (2.0 * here - born_old[strip(x, t, z), :]) + moved)
        return carry

    lax.fori_loop(0, CX, step, 0)
    add_sources(cells, amps, contrast, wave_part, born_part)
    take(rows_at, born, picks, rows, sums)
    lane = lax.broadcasted_iota(jnp.int32, (256, 128), 1)
    first[...] = jnp.where(lane < 4, jnp.sum(sums[...], axis=1, keepdims=True), 0.0) * slots[...]
    for copy in copies:
        copy.wait()


def fix(place, ends, parts, scales, x_halo, y_halo, outs, face, edges, middle, tiles=(0, 1)):
    wave_part, born_part = parts
    courant, contrast = scales
    wave, born, wave_rows, born_rows = outs
    sub, _ = iotas()
    even_x = place[0] == 0
    part = lax.bitwise_and(sub, 3)

    low_weights = [jnp.where(part < k, WEIGHTS[k - 1], 0.0) for k in range(1, 4)]
    high_weights = [jnp.where(part >= 4 - k, WEIGHTS[k - 1], 0.0) for k in range(1, 4)]

    def one(x, side, offset):
        for z in range(TZ):
            low, high = y_halo(x, z)
            wave_sums, born_sums = [None, None], [None, None]
            if low is not None:
                total = WEIGHTS[3] * low
                for k in range(1, 4):
                    total = total + low_weights[k - 1] * pltpu.roll(low, 4 + k, 0)
                wave_sums[0] = jnp.where(sub < 4, total, 0.0)
                born_sums[0] = jnp.where(sub < 4, pltpu.roll(total, 4, 0), 0.0)
            if high is not None:
                total = WEIGHTS[3] * high
                for k in range(1, 4):
                    total = total + high_weights[k - 1] * pltpu.roll(high, 4 - k, 0)
                wave_sums[1] = jnp.where(sub < 4, 0.0, pltpu.roll(total, 4, 0))
                born_sums[1] = jnp.where(sub < 4, 0.0, total)
            finals = {}
            for t in tiles:
                wave_sum, born_sum = wave_sums[t], born_sums[t]
                if side:
                    for m in range(4):
                        reach = offset + 4 - m if side < 0 else 4 - offset + m
                        if 1 <= reach <= 4:
                            lone, other = (x_halo[1], x_halo[0]) if side < 0 else x_halo
                            w = WEIGHTS[reach - 1] * ends[0 if side < 0 else 1]
                            wave_term = w * jnp.where(even_x, tile(lone, m, t, z), tile(other, m, t, z))
                            born_term = w * jnp.where(even_x, tile(lone, m + 4, t, z), tile(other, m + 4, t, z))
                            wave_sum = wave_term if wave_sum is None else wave_sum + wave_term
                            born_sum = born_term if born_sum is None else born_sum + born_term
                wave_value, born_value = tile(wave_part, x, t, z), tile(born_part, x, t, z)
                if wave_sum is not None:
                    speed = tile(courant, x, t, z)
                    moved = speed * wave_sum
                    wave_value = wave_value + moved
                    born_value = born_value + (tile(contrast, x, t, z) * moved + speed * born_sum)
                put(wave, x, t, z, wave_value)
                put(born, x, t, z, born_value)
                if wave_rows is not None:
                    wave_rows[strip(x, t, z), :] = wave_value
                born_rows[strip(x, t, z), :] = born_value
                finals[t] = (wave_value, born_value)
            if face is not None:
                ref, t = face
                wave_value, born_value = finals[t]
                if t == 0:
                    packed = jnp.where(sub < 4, wave_value, pltpu.roll(born_value, 4, 0))
                else:
                    packed = jnp.where(sub < 4, pltpu.roll(wave_value, 4, 0), born_value)
                put(ref, x, 0, z, packed)

    if edges:
        for x in range(4):
            one(x, -1, x)
        for x in range(CX - 4, CX):
            one(x, 1, x - (CX - 4))
    if middle:
        first, end = middle
        lax.fori_loop(first, end, lambda x, carry: (one(x, 0, 0), carry)[1], 0)


def low_side(face):
    return lambda x, z: (tile(face, x, 0, z), None)


def high_side(face):
    return lambda x, z: (None, tile(face, x, 0, z))


def fix_early(place, ends, parts, scales, rxa, rxb, rya, outs, ya):
    for even in (True, False):

        @pl.when((place[1] == 0) == even)
        def _():
            fix(
                place, ends, parts, scales, (rxa, rxb), high_side(rya) if even else low_side(rya), outs,
                None if ya is None else (ya, 1 if even else 0), True, (4, CX - 4),
            )


def fix_late(place, parts, scales, ryb, outs, yb):
    for even in (True, False):

        @pl.when((place[1] == 0) == even)
        def _():
            side = 0 if even else 1
            fix(
                place, None, parts, scales, None, low_side(ryb) if even else high_side(ryb), outs,
                None if yb is None else (yb, side), False, (0, CX), (side,),
            )


def early_first(
    place, ends, wave_part, born_part, courant, contrast, rxa, rxb, rya, wave, born, wave_rows, born_rows, ya,
):
    outs = (wave, born, wave_rows, born_rows)
    fix_early(place, ends, (wave_part, born_part), (courant, contrast), rxa, rxb, rya, outs, ya)


def late_first(
    place, wave_in, born_in, wave_rows_in, born_rows_in, courant, contrast, ryb,
    wave, born, wave_rows, born_rows, yb, xa, xb,
):
    outs = (wave, born, wave_rows, born_rows)
    fix_late(place, (wave_in, born_in), (courant, contrast), ryb, outs, yb)
    pack_x(place[0] == 0, xa, xb, wave, born)


def early_second(
    place, ends, wave_part, born_part, courant, contrast, rxa, rxb, rya, wave, born, born_rows,
):
    outs = (wave, born, None, born_rows)
    fix_early(place, ends, (wave_part, born_part), (courant, contrast), rxa, rxb, rya, outs, None)


def take(rows_at, grid, picks, rows, out):
    def step(g, carry):
        for half in range(2):
            for j in range(8):
                for t in range(8):
                    source = rows_at[g * 8 + (half * 1024 + t * 128 + j)]
                    rows[pl.ds(g * 64 + (half * 1024 + j * 8 + t), 1), :] = grid[pl.ds(source, 1), :]
        return carry

    lax.fori_loop(0, 16, step, 0)

    def total(g, carry):
        part = pl.ds(pl.multiple_of(g * 256, 256), 256)
        value = (rows[part, :] * picks[part, :]).reshape(32, 8, 128)
        out[pl.ds(pl.multiple_of(g * 32, 32), 32), :] = jnp.sum(value, axis=1)
        return carry

    lax.fori_loop(0, 8, total, 0)


def last_kernel(
    place, rows_at, wave_in, born_in, grid_in, courant, contrast, ryb, picks, first, slots, dest,
    wave, born, grid, wave_out, born_out, packed, rows, sums, sems,
):
    fix_late(place, (wave_in, born_in), (courant, contrast), ryb, (wave, born, None, grid), None)
    copies = [
        pltpu.make_async_copy(wave, wave_out, sems.at[0]),
        pltpu.make_async_copy(born, born_out, sems.at[1]),
    ]
    for copy in copies:
        copy.start()
    take(rows_at, grid, picks, rows, sums)
    two = jnp.sum(sums[...], axis=1, keepdims=True)
    lane = lax.broadcasted_iota(jnp.int32, (256, 128), 1)
    spread_out = first[...] + jnp.where(lane < 4, 0.0, two) * slots[...]
    owner = lax.broadcasted_iota(jnp.int32, (128, 256), 0)
    chosen = jnp.where(owner == dest[...], 1.0, 0.0).astype(F32)
    packed[...] = jnp.dot(chosen, spread_out, precision=lax.Precision.HIGHEST, preferred_element_type=F32)
    for copy in copies:
        copy.wait()


def pairs(count, first):
    found = []
    for i in range(first, count - 1, 2):
        found += [(i, i + 1), (i + 1, i)]
    return found


VM = pl.BlockSpec(memory_space=pltpu.VMEM)
SM = pl.BlockSpec(memory_space=pltpu.SMEM)
HB = pl.BlockSpec(memory_space=pltpu.HBM)


def kept(shape):
    return VM, pltpu.VMEM(shape, F32)


def plain(shape):
    return VM, jax.ShapeDtypeStruct(shape, F32)


def away(shape):
    return HB, jax.ShapeDtypeStruct(shape, F32)


def still(value):
    return pltpu.with_memory_space_constraint(value, pltpu.HBM)


def call(kernel, args, specs, outs, scratch, mib, us, aliases=None):
    return pl.pallas_call(
        kernel,
        out_shape=tuple(o[1] for o in outs),
        in_specs=specs,
        out_specs=tuple(o[0] for o in outs),
        scratch_shapes=list(scratch),
        input_output_aliases=aliases or {},
        compiler_params=pltpu.CompilerParams(vmem_limit_bytes=mib * 1024 * 1024),
        cost_estimate=pl.CostEstimate(flops=0, bytes_accessed=us * 3_000_000, transcendentals=0),
    )(*args)


def swap_x(xa, xb):
    flat = [(i * 16 + g, j * 16 + g) for i, j in pairs(8, 1) for g in range(16)]
    flat += [(i * 16 + g, i * 16 + (g ^ 1)) for i in (0, 7) for g in range(16)]
    rxb = lax.ppermute(xb, ("gx", "gy"), flat)
    rxa = lax.ppermute(xa, "gx", pairs(8, 0))
    return rxa, rxb


def swap_y(ya, yb):
    ryb = lax.ppermute(yb, "gy", pairs(16, 1))
    rya = lax.ppermute(ya, "gy", pairs(16, 0))
    return rya, ryb


def xy_table():
    size = CX * CY
    row = lax.broadcasted_iota(jnp.int32, (size, size), 0)
    col = lax.broadcasted_iota(jnp.int32, (size, size), 1)
    apart = jnp.abs(row - col)
    along_y = jnp.where(row // CY == col // CY, apart, 0)
    along_x = jnp.where(apart % CY == 0, apart // CY, 0)
    gap = jnp.maximum(along_x, along_y)
    table = jnp.zeros((size, size), F32)
    for k in range(1, 5):
        table = jnp.where(gap == k, WEIGHTS[k - 1], table)
    return table.astype(BF16)


def z_table():
    source = lax.broadcasted_iota(jnp.int32, (1024, 256), 0) % 512 - 128
    target = lax.broadcasted_iota(jnp.int32, (1024, 256), 1)
    gap = jnp.abs(source - target)
    table = jnp.zeros((1024, 256), F32)
    for k in range(1, 5):
        table = jnp.where(gap == k, WEIGHTS[k - 1], table)
    return table.astype(BF16)


def steps(
    wave_old,
    wave_now,
    born_old,
    born_now,
    courant,
    contrast,
    src_cell,
    src_amp,
    rcv_cell,
    rcv_weight,
    rcv_dest,
):
    index_x, index_y = lax.axis_index("gx"), lax.axis_index("gy")
    place = jnp.stack([index_x & 1, index_y & 1]).astype(jnp.int32)
    ends = jnp.stack([index_x > 0, index_x < 7]).astype(F32)
    field = pltpu.VMEM(BLOCK, F32)
    halves = [pltpu.VMEM((CX * CY, NZ + 256), BF16)] * 2 + [pltpu.VMEM((CX * CY, NZ), F32)] * 2
    x_faces, y_faces = [plain(XFACE)] * 2, [plain(YFACE)] * 2
    fixed = [kept(BLOCK)] * 2 + [kept((ROWS, 128))] * 2

    xa, xb, place, ends = call(
        edge_kernel, (place, ends, still(wave_now), still(born_now)), [SM, SM, HB, HB],
        x_faces + [(SM, jax.ShapeDtypeStruct((2,), jnp.int32)), (SM, jax.ShapeDtypeStruct((2,), F32))],
        [pltpu.SemaphoreType.DMA((2, 2))], 4, 1,
    )
    halo_x = swap_x(xa, xb)
    wave_rows, born_rows, ya, yb = call(
        pack_kernel, (place, wave_now, born_now), [SM, VM, VM],
        [kept((ROWS, 128))] * 2 + y_faces, [], 8, 2,
    )
    halo_y = swap_y(ya, yb)
    tables = (z_table(), xy_table())
    wave_part, born_part, speed, factor, picks = call(
        inner_first,
        (
            src_cell, src_amp[:, 0], wave_rows, born_rows, *tables, rcv_cell.T, rcv_weight.T,
            still(wave_old), still(born_old), still(courant), still(contrast),
        ),
        [SM, SM] + [VM] * 6 + [HB] * 4,
        [kept(BLOCK)] * 4 + [kept((2048, 128))], [field, field, *halves, pltpu.SemaphoreType.DMA((4,))], 14, 8,
    )

    cell = rcv_cell.T
    rows_at = (cell >> 14) * LAYER + ((cell >> 7) & 7) * STRIP + ((cell >> 10) & 15)
    rows_at = rows_at.reshape(8, 2, 128).transpose(1, 0, 2).reshape(2048)
    dest = rcv_dest[:, 0]
    order = jnp.arange(256, dtype=jnp.int32)
    earlier = (dest[:, None] == dest[None, :]) & (order[None, :] < order[:, None])
    slot = jnp.sum(earlier.astype(jnp.int32), axis=1)
    lane = lax.broadcasted_iota(jnp.int32, (256, 128), 1)
    slots = jnp.where((lane < 8) & (lane % 4 == slot[:, None]), 1.0, 0.0).astype(F32)

    *mid, ya = call(
        early_first, (place, ends, wave_part, born_part, speed, factor, *halo_x, halo_y[0]),
        [SM] * 2 + [VM] * 7, fixed + y_faces[:1], [], 4, 3, {2: 0, 3: 1},
    )
    wave_mid, born_mid, wave_mid_rows, born_mid_rows, yb, xa, xb = call(
        late_first, (place, *mid, speed, factor, halo_y[1]),
        [SM] + [VM] * 7, fixed + y_faces[:1] + x_faces, [], 4, 2, {i + 1: i for i in range(4)},
    )
    next_x = swap_x(xa, xb)
    next_y = swap_y(ya, yb)
    wave_part, born_part, first, wave_next, born_next = call(
        inner_second,
        (
            src_cell, src_amp[:, 1], rows_at, wave_mid_rows, born_mid_rows, *tables, wave_rows, born_rows,
            speed, factor, picks, slots, wave_mid, born_mid,
        ),
        [SM] * 3 + [VM] * 12,
        [kept(BLOCK)] * 2 + [plain((256, 128)), away(BLOCK), away(BLOCK)],
        [*halves, pltpu.VMEM((2048, 128), F32), pltpu.VMEM((256, 128), F32), pltpu.SemaphoreType.DMA((2,))], 12, 10,
    )
    near = call(
        early_second, (place, ends, wave_part, born_part, speed, factor, *next_x, next_y[0]),
        [SM] * 2 + [VM] * 7, [kept(BLOCK)] * 2 + [kept((ROWS, 128))], [], 4, 3, {2: 0, 3: 1},
    )
    *_, wave_last, born_last, packed = call(
        last_kernel,
        (place, rows_at, *near, speed, factor, next_y[1], picks, first, slots, dest[None, :]),
        [SM] * 2 + [VM] * 10,
        [kept(BLOCK)] * 2 + [kept((ROWS, 128)), away(BLOCK), away(BLOCK), plain((128, 128))],
        [pltpu.VMEM((2048, 128), F32), pltpu.VMEM((256, 128), F32), pltpu.SemaphoreType.DMA((2,))],
        8, 4, {2: 0, 3: 1, 4: 2},
    )
    arrived = lax.all_to_all(
        packed.reshape(128, 1, 128), ("gx", "gy"), split_axis=0, concat_axis=0, tiled=True
    )
    gathers = arrived[:, 0, :8].reshape(1, 128, 2, CAP)
    return (wave_next, wave_last, born_next, born_last, gathers)


def solution(mesh):
    placed = (P("gx", "gy", None),) * 6 + (
        P(("gx", "gy")),
        P(("gx", "gy"), None),
        P(("gx", "gy"), None),
        P(("gx", "gy"), None),
        P(("gx", "gy"), None),
    )
    return jax.shard_map(
        steps,
        mesh=mesh,
        in_specs=placed,
        out_specs=(P("gx", "gy", None),) * 4 + (P(("gx", "gy"), None, None, None),),
        check_vma=False,
    )
```

```python
import jax
import jax.numpy as jnp
from jax import lax
from jax.experimental import pallas as pl
from jax.experimental.pallas import tpu as pltpu
from jax.sharding import PartitionSpec as P


CAP = 4
SCALE = 5040.0
CENTER = -3.0 * 14350.0
WEIGHTS = (8064.0, -1008.0, 128.0, -9.0)
CX, CY, NZ = 32, 16, 1024
TZ = NZ // 128
BLOCK = (CX, CY, NZ)
XFACE = (8, CY, NZ)
YFACE = (CX, 8, NZ)
STRIP = CY
LAYER = TZ * STRIP
ROWS = CX * LAYER
F32 = jnp.float32
BF16 = jnp.bfloat16


def iotas():
    sub = lax.broadcasted_iota(jnp.int32, (8, 128), 0)
    lane = lax.broadcasted_iota(jnp.int32, (8, 128), 1)
    return sub, lane


def tile(ref, x, t, z):
    return ref[x, t * 8 : t * 8 + 8, z * 128 : z * 128 + 128]


def put(ref, x, t, z, value):
    ref[x, t * 8 : t * 8 + 8, z * 128 : z * 128 + 128] = value


def strip(x, t, z):
    return pl.ds(pl.multiple_of(x * LAYER + (z * STRIP + t * 8), 8), 8)


def pack_y(sub, even, ya, yb, x, z, w0, w1, b0, b1):
    low = jnp.where(sub < 4, w0, pltpu.roll(b0, 4, 0))
    high = jnp.where(sub < 4, pltpu.roll(w1, 4, 0), b1)
    put(ya, x, 0, z, jnp.where(even, high, low))
    put(yb, x, 0, z, jnp.where(even, low, high))


def pack_x(even, xa, xb, wave, born):
    start_a = jnp.where(even, CX - 4, 0)
    start_b = jnp.where(even, 0, CX - 4)
    for i in range(4):
        xa[i] = wave[start_a + i]
        xa[i + 4] = born[start_a + i]
        xb[i] = wave[start_b + i]
        xb[i + 4] = born[start_b + i]


def edge_kernel(place, ends, wave, born, xa, xb, place_out, ends_out, sems):
    for i in range(2):
        place_out[i] = place[i]
        ends_out[i] = ends[i]
    even = place[0] == 0
    starts = (jnp.where(even, CX - 4, 0), jnp.where(even, 0, CX - 4))
    copies = [
        pltpu.make_async_copy(field.at[pl.ds(start, 4)], face.at[pl.ds(4 * i, 4)], sems.at[j, i])
        for j, (start, face) in enumerate(zip(starts, (xa, xb)))
        for i, field in enumerate((wave, born))
    ]
    for copy in copies:
        copy.start()
    for copy in copies:
        copy.wait()


def pack_kernel(place, wave, born, wave_rows, born_rows, ya, yb):
    sub, _ = iotas()
    even_y = place[1] == 0

    def step(x, carry):
        for z in range(TZ):
            w0, w1, b0, b1 = tile(wave, x, 0, z), tile(wave, x, 1, z), tile(born, x, 0, z), tile(born, x, 1, z)
            pack_y(sub, even_y, ya, yb, x, z, w0, w1, b0, b1)
            wave_rows[strip(x, 0, z), :] = w0
            wave_rows[strip(x, 1, z), :] = w1
            born_rows[strip(x, 0, z), :] = b0
            born_rows[strip(x, 1, z), :] = b1
        return carry

    lax.fori_loop(0, CX, step, 0)


def stencil(ref, high, low, z_weights, xy_weights, out):
    zero = jnp.zeros((CX * CY, 128), BF16)
    for half in (high, low):
        half[:, 0:128] = zero
        half[:, 128 + NZ : 256 + NZ] = zero

    def split(x, carry):
        rows = pl.ds(pl.multiple_of(x * CY, CY), CY)
        for z in range(TZ):
            value = ref[pl.ds(pl.multiple_of(x * LAYER + z * STRIP, CY), CY), :]
            top = value.astype(BF16)
            high[rows, 128 + z * 128 : 256 + z * 128] = top
            low[rows, 128 + z * 128 : 256 + z * 128] = (value - top.astype(F32)).astype(BF16)
        return carry

    lax.fori_loop(0, CX, split, 0, unroll=2)
    for c in range(NZ // 256):
        window = slice(c * 256, c * 256 + 512)
        inside = slice(c * 256 + 128, c * 256 + 384)
        wide = jnp.concatenate([high[:, window], low[:, window]], axis=1)
        tall = jnp.concatenate([high[:, inside], low[:, inside]], axis=0)
        twice = jnp.concatenate([xy_weights[...], xy_weights[...]], axis=1)
        out[:, c * 256 : c * 256 + 256] = jnp.dot(wide, z_weights[...], preferred_element_type=F32) + jnp.dot(
            twice, tall, preferred_element_type=F32
        )


def spread(ref, around, x, t, z):
    here = ref[strip(x, t, z), :]
    total = CENTER * here + around[pl.ds(pl.multiple_of(x * CY + t * 8, 8), 8), z * 128 : z * 128 + 128]
    return here, total


def add_sources(cells, amps, contrast, wave_part, born_part):
    sub, lane = iotas()
    for i in range(4):
        cell = cells[i]
        x = lax.shift_right_logical(cell, 14)
        y = lax.bitwise_and(lax.shift_right_logical(cell, 10), 15)
        z = lax.bitwise_and(cell, NZ - 1)
        row = pl.multiple_of(lax.bitwise_and(y, 8), 8)
        col = pl.multiple_of(lax.bitwise_and(z, NZ - 128), 128)
        here = (sub == lax.bitwise_and(y, 7)) & (lane == lax.bitwise_and(z, 127))
        added = jnp.where(here, amps[i], 0.0)
        at = (x, pl.ds(row, 8), pl.ds(col, 128))
        wave_part[at] = wave_part[at] + added
        born_part[at] = born_part[at] + contrast[at] * added


def make_picks(taps, weights, picks):
    lane = lax.broadcasted_iota(jnp.int32, (8, 128), 1)
    for half in range(2):
        spots = lax.bitwise_and(taps[:, half * 128 : half * 128 + 128], 127)
        gains = weights[:, half * 128 : half * 128 + 128]

        def group(g, carry):
            spots, gains = carry
            for j in range(16):
                row = pl.multiple_of((half * 128 + g * 16 + j) * 8, 8)
                picks[pl.ds(row, 8), :] = jnp.where(lane == spots[:, j : j + 1], gains[:, j : j + 1], 0.0)
            return pltpu.roll(spots, 112, 1), pltpu.roll(gains, 112, 1)

        lax.fori_loop(0, 8, group, (spots, gains))


def inner_first(
    cells, amps, wave, born, z_weights, xy_weights, taps, weights, wave_old_in, born_old_in, courant_in, contrast_in,
    wave_part, born_part, courant, contrast, picks, wave_old, born_old, high, low, wave_sum_all, born_sum_all, sems,
):
    copies = [
        pltpu.make_async_copy(a, b, sems.at[i])
        for i, (a, b) in enumerate(
            ((wave_old_in, wave_old), (born_old_in, born_old), (courant_in, courant), (contrast_in, contrast))
        )
    ]
    for copy in copies:
        copy.start()
    stencil(wave, high, low, z_weights, xy_weights, wave_sum_all)
    stencil(born, high, low, z_weights, xy_weights, born_sum_all)
    make_picks(taps, weights, picks)
    for copy in copies:
        copy.wait()

    def step(x, carry):
        for z in range(TZ):
            for t in range(2):
                speed = tile(courant, x, t, z) * (1.0 / SCALE)
                put(courant, x, t, z, speed)
                here, total = spread(wave, wave_sum_all, x, t, z)
                moved = speed * total
                put(wave_part, x, t, z, (2.0 * here - tile(wave_old, x, t, z)) + moved)
                here, total = spread(born, born_sum_all, x, t, z)
                moved = speed * total + tile(contrast, x, t, z) * moved
                put(born_part, x, t, z, (2.0 * here - tile(born_old, x, t, z)) + moved)
        return carry

    lax.fori_loop(0, CX, step, 0)
    add_sources(cells, amps, contrast, wave_part, born_part)


def inner_second(
    cells, amps, rows_at, wave, born, z_weights, xy_weights, wave_old, born_old, courant, contrast, picks, slots, wave_now, born_now,
    wave_part, born_part, first, wave_out, born_out, high, low, wave_sum_all, born_sum_all, rows, sums, sems,
):
    copies = [
        pltpu.make_async_copy(wave_now, wave_out, sems.at[0]),
        pltpu.make_async_copy(born_now, born_out, sems.at[1]),
    ]
    for copy in copies:
        copy.start()
    stencil(wave, high, low, z_weights, xy_weights, wave_sum_all)
    stencil(born, high, low, z_weights, xy_weights, born_sum_all)

    def step(x, carry):
        for z in range(TZ):
            for t in range(2):
                speed = tile(courant, x, t, z)
                here, total = spread(wave, wave_sum_all, x, t, z)
                moved = speed * total
                put(wave_part, x, t, z, (2.0 * here - wave_old[strip(x, t, z), :]) + moved)
                here, total = spread(born, born_sum_all, x, t, z)
                moved = speed * total + tile(contrast, x, t, z) * moved
                put(born_part, x, t, z, (2.0 * here - born_old[strip(x, t, z), :]) + moved)
        return carry

    lax.fori_loop(0, CX, step, 0)
    add_sources(cells, amps, contrast, wave_part, born_part)
    take(rows_at, born, picks, rows, sums)
    lane = lax.broadcasted_iota(jnp.int32, (256, 128), 1)
    first[...] = jnp.where(lane < 4, jnp.sum(sums[...], axis=1, keepdims=True), 0.0) * slots[...]
    for copy in copies:
        copy.wait()


def fix(place, ends, parts, scales, x_halo, y_halo, outs, y_faces, edges, middle, tiles=(0, 1)):
    wave_part, born_part = parts
    courant, contrast = scales
    wave, born, wave_rows, born_rows = outs
    sub, _ = iotas()
    even_x = place[0] == 0
    even_y = place[1] == 0
    part = lax.bitwise_and(sub, 3)

    low_weights = [jnp.where(part < k, WEIGHTS[k - 1], 0.0) for k in range(1, 4)]
    high_weights = [jnp.where(part >= 4 - k, WEIGHTS[k - 1], 0.0) for k in range(1, 4)]

    def one(x, side, offset):
        for z in range(TZ):
            low, high = y_halo(x, z)
            wave_sums, born_sums = [None, None], [None, None]
            if low is not None:
                total = WEIGHTS[3] * low
                for k in range(1, 4):
                    total = total + low_weights[k - 1] * pltpu.roll(low, 4 + k, 0)
                wave_sums[0] = jnp.where(sub < 4, total, 0.0)
                born_sums[0] = jnp.where(sub < 4, pltpu.roll(total, 4, 0), 0.0)
            if high is not None:
                total = WEIGHTS[3] * high
                for k in range(1, 4):
                    total = total + high_weights[k - 1] * pltpu.roll(high, 4 - k, 0)
                wave_sums[1] = jnp.where(sub < 4, 0.0, pltpu.roll(total, 4, 0))
                born_sums[1] = jnp.where(sub < 4, 0.0, total)
            finals = []
            for t in tiles:
                wave_sum, born_sum = wave_sums[t], born_sums[t]
                if side:
                    for m in range(4):
                        reach = offset + 4 - m if side < 0 else 4 - offset + m
                        if 1 <= reach <= 4:
                            lone, other = (x_halo[1], x_halo[0]) if side < 0 else x_halo
                            w = WEIGHTS[reach - 1] * ends[0 if side < 0 else 1]
                            wave_term = w * jnp.where(even_x, tile(lone, m, t, z), tile(other, m, t, z))
                            born_term = w * jnp.where(even_x, tile(lone, m + 4, t, z), tile(other, m + 4, t, z))
                            wave_sum = wave_term if wave_sum is None else wave_sum + wave_term
                            born_sum = born_term if born_sum is None else born_sum + born_term
                wave_value, born_value = tile(wave_part, x, t, z), tile(born_part, x, t, z)
                if wave_sum is not None:
                    speed = tile(courant, x, t, z)
                    moved = speed * wave_sum
                    wave_value = wave_value + moved
                    born_value = born_value + (tile(contrast, x, t, z) * moved + speed * born_sum)
                put(wave, x, t, z, wave_value)
                put(born, x, t, z, born_value)
                if wave_rows is not None:
                    wave_rows[strip(x, t, z), :] = wave_value
                born_rows[strip(x, t, z), :] = born_value
                finals.append((wave_value, born_value))
            if y_faces is not None:
                (w0, b0), (w1, b1) = finals
                pack_y(sub, even_y, *y_faces, x, z, w0, w1, b0, b1)

    if edges:
        for x in range(4):
            one(x, -1, x)
        for x in range(CX - 4, CX):
            one(x, 1, x - (CX - 4))
    if middle:
        first, end = middle
        unroll = 2 if len(tiles) == 1 else 1
        lax.fori_loop(first, end, lambda x, carry: (one(x, 0, 0), carry)[1], 0, unroll=unroll)


def both_sides(place, ya, yb):
    even_y = place[1] == 0

    def pick(x, z):
        from_a, from_b = tile(ya, x, 0, z), tile(yb, x, 0, z)
        return jnp.where(even_y, from_b, from_a), jnp.where(even_y, from_a, from_b)

    return pick


def low_side(face):
    return lambda x, z: (tile(face, x, 0, z), None)


def high_side(face):
    return lambda x, z: (None, tile(face, x, 0, z))


def fix_edges(
    place, ends, wave_part, born_part, courant, contrast, rxa, rxb, rya, ryb,
    wave, born, wave_rows, born_rows, ya, yb, xa, xb,
):
    fix(
        place, ends, (wave_part, born_part), (courant, contrast), (rxa, rxb), both_sides(place, rya, ryb),
        (wave, born, wave_rows, born_rows), (ya, yb), True, None,
    )
    pack_x(place[0] == 0, xa, xb, wave, born)


def fix_middle(
    place, ends, wave_part, born_part, courant, contrast, rya, ryb, wave_in, born_in, rows_a, rows_b, ya_in, yb_in,
    wave, born, wave_rows, born_rows, ya, yb,
):
    fix(
        place, ends, (wave_part, born_part), (courant, contrast), None, both_sides(place, rya, ryb),
        (wave, born, wave_rows, born_rows), (ya, yb), False, (4, CX - 4),
    )


def fix_early(
    place, ends, wave_part, born_part, courant, contrast, rxa, rxb, rya, wave, born, born_rows,
):
    for even in (True, False):

        @pl.when((place[1] == 0) == even)
        def _():
            fix(
                place, ends, (wave_part, born_part), (courant, contrast), (rxa, rxb),
                high_side(rya) if even else low_side(rya),
                (wave, born, None, born_rows), None, True, (4, CX - 4),
            )


def take(rows_at, grid, picks, rows, out):
    for r in range(256):
        for t in range(8):
            source = rows_at[r // 128 * 1024 + t * 128 + r % 128]
            rows[r * 8 + t : r * 8 + t + 1, :] = grid[pl.ds(source, 1), :]

    def total(g, carry):
        part = pl.ds(pl.multiple_of(g * 256, 256), 256)
        value = (rows[part, :] * picks[part, :]).reshape(32, 8, 128)
        out[pl.ds(pl.multiple_of(g * 32, 32), 32), :] = jnp.sum(value, axis=1)
        return carry

    lax.fori_loop(0, 8, total, 0)


def last_kernel(
    place, rows_at, wave_in, born_in, grid_in, courant, contrast, ryb, picks, first, slots, dest,
    wave, born, grid, wave_out, born_out, packed, rows, sums, sems,
):
    for even in (True, False):

        @pl.when((place[1] == 0) == even)
        def _():
            fix(
                place, None, (wave_in, born_in), (courant, contrast), None,
                low_side(ryb) if even else high_side(ryb),
                (wave, born, None, grid), None, False, (0, CX), (0,) if even else (1,),
            )

    copies = [
        pltpu.make_async_copy(wave, wave_out, sems.at[0]),
        pltpu.make_async_copy(born, born_out, sems.at[1]),
    ]
    for copy in copies:
        copy.start()
    take(rows_at, grid, picks, rows, sums)
    two = jnp.sum(sums[...], axis=1, keepdims=True)
    lane = lax.broadcasted_iota(jnp.int32, (256, 128), 1)
    spread_out = first[...] + jnp.where(lane < 4, 0.0, two) * slots[...]
    owner = lax.broadcasted_iota(jnp.int32, (128, 256), 0)
    chosen = jnp.where(owner == dest[...], 1.0, 0.0).astype(BF16)
    pieces = []
    for _ in range(3):
        pieces.append(spread_out.astype(BF16))
        spread_out = spread_out - pieces[-1].astype(F32)
    packed[...] = jnp.dot(
        jnp.concatenate([chosen] * 3, axis=1), jnp.concatenate(pieces, axis=0), preferred_element_type=F32
    )
    for copy in copies:
        copy.wait()


def pairs(count, first):
    found = []
    for i in range(first, count - 1, 2):
        found += [(i, i + 1), (i + 1, i)]
    return found


VM = pl.BlockSpec(memory_space=pltpu.VMEM)
SM = pl.BlockSpec(memory_space=pltpu.SMEM)
HB = pl.BlockSpec(memory_space=pltpu.HBM)


def kept(shape):
    return VM, pltpu.VMEM(shape, F32)


def plain(shape):
    return VM, jax.ShapeDtypeStruct(shape, F32)


def away(shape):
    return HB, jax.ShapeDtypeStruct(shape, F32)


def still(value):
    return pltpu.with_memory_space_constraint(value, pltpu.HBM)


def call(kernel, args, specs, outs, scratch, mib, us, aliases=None):
    return pl.pallas_call(
        kernel,
        out_shape=tuple(o[1] for o in outs),
        in_specs=specs,
        out_specs=tuple(o[0] for o in outs),
        scratch_shapes=list(scratch),
        input_output_aliases=aliases or {},
        compiler_params=pltpu.CompilerParams(vmem_limit_bytes=mib * 1024 * 1024),
        cost_estimate=pl.CostEstimate(flops=0, bytes_accessed=us * 3_000_000, transcendentals=0),
    )(*args)


def swap_x(xa, xb):
    flat = [(i * 16 + g, j * 16 + g) for i, j in pairs(8, 1) for g in range(16)]
    flat += [(i * 16 + g, i * 16 + (g ^ 1)) for i in (0, 7) for g in range(16)]
    rxb = lax.ppermute(xb, ("gx", "gy"), flat)
    rxa = lax.ppermute(xa, "gx", pairs(8, 0))
    return rxa, rxb


def swap_y(ya, yb):
    ryb = lax.ppermute(yb, "gy", pairs(16, 1))
    rya = lax.ppermute(ya, "gy", pairs(16, 0))
    return rya, ryb


def xy_table():
    size = CX * CY
    row = lax.broadcasted_iota(jnp.int32, (size, size), 0)
    col = lax.broadcasted_iota(jnp.int32, (size, size), 1)
    apart = jnp.abs(row - col)
    along_y = jnp.where(row // CY == col // CY, apart, 0)
    along_x = jnp.where(apart % CY == 0, apart // CY, 0)
    gap = jnp.maximum(along_x, along_y)
    table = jnp.zeros((size, size), F32)
    for k in range(1, 5):
        table = jnp.where(gap == k, WEIGHTS[k - 1], table)
    return table.astype(BF16)


def z_table():
    source = lax.broadcasted_iota(jnp.int32, (1024, 256), 0) % 512 - 128
    target = lax.broadcasted_iota(jnp.int32, (1024, 256), 1)
    gap = jnp.abs(source - target)
    table = jnp.zeros((1024, 256), F32)
    for k in range(1, 5):
        table = jnp.where(gap == k, WEIGHTS[k - 1], table)
    return table.astype(BF16)


def steps(
    wave_old,
    wave_now,
    born_old,
    born_now,
    courant,
    contrast,
    src_cell,
    src_amp,
    rcv_cell,
    rcv_weight,
    rcv_dest,
):
    index_x, index_y = lax.axis_index("gx"), lax.axis_index("gy")
    place = jnp.stack([index_x & 1, index_y & 1]).astype(jnp.int32)
    ends = jnp.stack([index_x > 0, index_x < 7]).astype(F32)
    field = pltpu.VMEM(BLOCK, F32)
    halves = [pltpu.VMEM((CX * CY, NZ + 256), BF16)] * 2 + [pltpu.VMEM((CX * CY, NZ), F32)] * 2
    x_faces, y_faces = [plain(XFACE)] * 2, [plain(YFACE)] * 2
    fixed = [kept(BLOCK)] * 2 + [kept((ROWS, 128))] * 2

    xa, xb, place, ends = call(
        edge_kernel, (place, ends, still(wave_now), still(born_now)), [SM, SM, HB, HB],
        x_faces + [(SM, jax.ShapeDtypeStruct((2,), jnp.int32)), (SM, jax.ShapeDtypeStruct((2,), F32))],
        [pltpu.SemaphoreType.DMA((2, 2))], 4, 1,
    )
    halo_x = swap_x(xa, xb)
    wave_rows, born_rows, ya, yb = call(
        pack_kernel, (place, wave_now, born_now), [SM, VM, VM],
        [kept((ROWS, 128))] * 2 + y_faces, [], 8, 2,
    )
    halo_y = swap_y(ya, yb)
    tables = (z_table(), xy_table())
    wave_part, born_part, speed, factor, picks = call(
        inner_first,
        (
            src_cell, src_amp[:, 0], wave_rows, born_rows, *tables, rcv_cell.T, rcv_weight.T,
            still(wave_old), still(born_old), still(courant), still(contrast),
        ),
        [SM, SM] + [VM] * 6 + [HB] * 4,
        [kept(BLOCK)] * 4 + [kept((2048, 128))], [field, field, *halves, pltpu.SemaphoreType.DMA((4,))], 14, 8,
    )

    cell = rcv_cell.T
    rows_at = (cell >> 14) * LAYER + ((cell >> 7) & 7) * STRIP + ((cell >> 10) & 15)
    rows_at = rows_at.reshape(8, 2, 128).transpose(1, 0, 2).reshape(2048)
    dest = rcv_dest[:, 0]
    order = jnp.arange(256, dtype=jnp.int32)
    earlier = (dest[:, None] == dest[None, :]) & (order[None, :] < order[:, None])
    slot = jnp.sum(earlier.astype(jnp.int32), axis=1)
    lane = lax.broadcasted_iota(jnp.int32, (256, 128), 1)
    slots = jnp.where((lane < 8) & (lane % 4 == slot[:, None]), 1.0, 0.0).astype(F32)

    shared = (wave_part, born_part, speed, factor)
    *mid, xa, xb = call(
        fix_edges, (place, ends, *shared, *halo_x, *halo_y),
        [SM] * 2 + [VM] * 8, fixed + y_faces + x_faces, [], 4, 2,
    )
    next_x = swap_x(xa, xb)
    wave_mid, born_mid, wave_mid_rows, born_mid_rows, ya, yb = call(
        fix_middle, (place, ends, *shared, *halo_y, *mid),
        [SM] * 2 + [VM] * 12, fixed + y_faces, [], 4, 2, {i + 8: i for i in range(6)},
    )
    next_y = swap_y(ya, yb)
    wave_part, born_part, first, wave_next, born_next = call(
        inner_second,
        (
            src_cell, src_amp[:, 1], rows_at, wave_mid_rows, born_mid_rows, *tables, wave_rows, born_rows,
            speed, factor, picks, slots, wave_mid, born_mid,
        ),
        [SM] * 3 + [VM] * 12,
        [kept(BLOCK)] * 2 + [plain((256, 128)), away(BLOCK), away(BLOCK)],
        [*halves, pltpu.VMEM((2048, 128), F32), pltpu.VMEM((256, 128), F32), pltpu.SemaphoreType.DMA((2,))], 12, 10,
    )
    near = call(
        fix_early, (place, ends, wave_part, born_part, speed, factor, *next_x, next_y[0]),
        [SM] * 2 + [VM] * 7, [kept(BLOCK)] * 2 + [kept((ROWS, 128))], [], 4, 3, {2: 0, 3: 1},
    )
    *_, wave_last, born_last, packed = call(
        last_kernel,
        (place, rows_at, *near, speed, factor, next_y[1], picks, first, slots, dest[None, :]),
        [SM] * 2 + [VM] * 10,
        [kept(BLOCK)] * 2 + [kept((ROWS, 128)), away(BLOCK), away(BLOCK), plain((128, 128))],
        [pltpu.VMEM((2048, 128), F32), pltpu.VMEM((256, 128), F32), pltpu.SemaphoreType.DMA((2,))],
        8, 4, {2: 0, 3: 1, 4: 2},
    )
    arrived = lax.all_to_all(
        packed.reshape(128, 1, 128), ("gx", "gy"), split_axis=0, concat_axis=0, tiled=True
    )
    gathers = arrived[:, 0, :8].reshape(1, 128, 2, CAP)
    return (wave_next, wave_last, born_next, born_last, gathers)


def solution(mesh):
    placed = (P("gx", "gy", None),) * 6 + (
        P(("gx", "gy")),
        P(("gx", "gy"), None),
        P(("gx", "gy"), None),
        P(("gx", "gy"), None),
        P(("gx", "gy"), None),
    )
    return jax.shard_map(
        steps,
        mesh=mesh,
        in_specs=placed,
        out_specs=(P("gx", "gy", None),) * 4 + (P(("gx", "gy"), None, None, None),),
        check_vma=False,
    )
```
